256 devices in a mesh: batch: 8 (over z), queue: 32 (over x, y, core).
Axes of the slice: x: 4, y: 4, z: 8, core: 2. Of those that a mesh axis runs over, the one named last changes fastest.
Arguments:
- key_inputs: bfloat16 [8192, 1024], P('batch'), may hold values from -6 to 6
- head_in: bfloat16 [4096, 1024], P('queue'), may hold values from -0.1875 to 0.1875
- head_out: bfloat16 [4096, 1024], P('queue'), may hold values from -0.09375 to 0.09375
- queue_keys: bfloat16 [131072, 1024], P('queue'), may hold values from -1 to 1
- slots: int32 [8192], replicated, may hold values from 0 to 131071, as said below
- questions: bfloat16 [4096, 1024], P(('batch', 'queue')), may hold values from -4 to 4
- positives: int32 [4096], P('batch'), may hold values from 0 to 131071
Outputs:
- queue_out: bfloat16 [131072, 1024], P('queue')
- loss: float32 [], replicated
- question_grads: float32 [4096, 1024], P(('batch', 'queue'))
The draws below stay inside these ranges and needn't reach their ends.
Inputs may be any that keep to these rules, and one draw needn't show every extreme that they name: The 8192 slots are distinct. In each aligned block of 32 rows, exactly 1 row name slots in each range o * 4096 to o * 4096 + 4095.
All inputs are finite; a program needn't handle non-finite values.
Results may differ from the reference program's by a relative error of at most 0.0025.
Values may be sent and summed in bfloat16 or wider, within the bound.
A program may use at most 128 MiB of HBM per device.

```python
import jax
import jax.numpy as jnp
from jax import lax

D = 1024
FF = 4096
KEY_DEV = 32
SEG_DEV = 4096
NEWK = 8192
QLEN = 131072
QUES = 4096
PER_OWNER = 1
N_BATCH = 8
N_QUEUE = 32


aligned_count = 8


def slot_table(key):
    table_key = jax.random.fold_in(key, 101)
    spot_key, shuffle_key = jax.random.split(table_key)
    pick_key = jax.random.fold_in(table_key, 7)
    middle = jnp.tile(jnp.arange(1, SEG_DEV - 1, dtype=jnp.int32)[None, :], (N_QUEUE, 1))
    middle = jax.random.permutation(spot_key, middle, axis=1, independent=True)
    ends = jnp.tile(jnp.array([0, SEG_DEV - 1], jnp.int32)[None, :], (N_QUEUE, 1))
    spots = jnp.concatenate([ends, middle], axis=1)[:, :KEY_DEV * N_BATCH]
    spots = jax.random.permutation(pick_key, spots, axis=1, independent=True)
    spots = spots.reshape(N_QUEUE, N_BATCH * N_QUEUE, PER_OWNER)
    spots = spots + (jnp.arange(N_QUEUE, dtype=jnp.int32) * SEG_DEV)[:, None, None]
    spots = jnp.transpose(spots, (1, 0, 2)).reshape(N_BATCH * N_QUEUE, KEY_DEV)
    spots = jax.random.permutation(shuffle_key, spots, axis=1, independent=True)
    return spots.reshape(NEWK)


def aligned_parts(key):
    slot_values = slot_table(key)
    taken = jnp.zeros((QLEN,), jnp.int32).at[slot_values].set(1)
    free_slots = jnp.argsort(taken, stable=True)
    picks = jax.random.permutation(jax.random.fold_in(key, 202), QLEN - NEWK)[:2 * aligned_count]
    chosen = free_slots[picks]
    signs = jnp.where(jax.random.uniform(jax.random.fold_in(key, 204), (2 * aligned_count, D)) < 0.5, -1.0, 1.0)
    half_width = D // 2
    lower = (jnp.arange(D, dtype=jnp.int32) < half_width).astype(jnp.float32)
    masks = jnp.concatenate([jnp.tile(lower[None, :], (aligned_count, 1)), jnp.tile(1.0 - lower[None, :], (aligned_count, 1))], axis=0)
    vectors = signs * masks * (1.0 / half_width) ** 0.5
    return (chosen, vectors)


def draw_slots(key, part):
    return slot_table(key)


def draw_queue_keys(key, part):
    value_key = jax.random.fold_in(key, 301)
    table = jnp.clip(jax.random.normal(value_key, (QLEN, D), jnp.float32), -6.0, 6.0) / D ** 0.5
    chosen, vectors = aligned_parts(key)
    return table.at[chosen].set(vectors).astype(jnp.bfloat16)


def draw_questions(key, part):
    value_key = jax.random.fold_in(key, 401)
    jitter_key = jax.random.fold_in(key, 402)
    ramp = 0.02 * 16.0 ** (jnp.arange(QUES, dtype=jnp.float32) / QUES)
    jitter = jnp.exp(jax.random.uniform(jitter_key, (QUES,), jnp.float32, 0.0, 0.6931))
    row_scale = (ramp * jitter)[:, None]
    table = row_scale * jnp.clip(jax.random.normal(value_key, (QUES, D), jnp.float32), -6.0, 6.0)
    return table.astype(jnp.bfloat16)


def place_ends(entries, stream_key, least, high):
    dims = entries.shape
    place = [jax.random.randint(jax.random.fold_in(stream_key, axis), (), 0, dims[axis]) for axis in range(len(dims))]
    entries = entries.at[tuple(place)].set(least)
    longest = dims.index(max(dims))
    place[longest] = (place[longest] + 1) % dims[longest]
    return entries.at[tuple(place)].set(high)


def steps_of(key, extent, pieces, low, largest):
    def one(position, parts):
        heights = jax.random.uniform(jax.random.fold_in(jax.random.fold_in(key, 6), position), (parts,), jnp.float32, low / len(pieces), largest / len(pieces))
        return jnp.repeat(jnp.exp(heights), extent[position] // parts).reshape((-1,) + (1,) * (len(extent) - position - 1))

    loudness = one(*pieces[0])
    for cut in pieces[1:]:
        loudness = loudness * one(*cut)
    return loudness


def gaussian(own_key, dims, spread, most, pieces=(), held_as=jnp.bfloat16):
    values = spread * jax.random.normal(own_key, dims, jnp.float32)
    if pieces:
        values = values * steps_of(own_key, dims, pieces, -0.22, 0.18)
    return jnp.clip(values, -most, most).astype(held_as)


def setup_inputs(seed: int = 0) -> dict:
    arg_keys = jax.random.split(jax.random.key(seed), 8)
    return {
        "key_inputs": gaussian(arg_keys[0], (NEWK, D), 1.0, 6.0, ((0, 8),)),
        "head_in": gaussian(arg_keys[1], (FF, D), D ** -0.5, 0.1875, ((0, 32),)),
        "head_out": gaussian(arg_keys[2], (FF, D), FF ** -0.5, 0.09375, ((0, 32),)),
        "queue_keys": draw_queue_keys(jax.random.fold_in(arg_keys[7], 71), 0),
        "slots": draw_slots(jax.random.fold_in(arg_keys[7], 71), 0),
        "questions": draw_questions(jax.random.fold_in(arg_keys[7], 71), 0),
        "positives": place_ends(jax.random.randint(arg_keys[6], (QUES,), 0, QLEN), jax.random.fold_in(arg_keys[6], 1), 0, QLEN - 1).astype(jnp.int32),
    }


inverse_temp = 20.0
epsilon = 1e-06

def encode_keys(key_inputs, head_in, head_out):
    group_size = FF // N_QUEUE
    first_groups = head_in.reshape(N_QUEUE, group_size, D)
    second_groups = head_out.reshape(N_QUEUE, group_size, D)

    def one_group(running, pair):
        first_part, second_part = pair
        hidden = jax.nn.gelu(jnp.dot(key_inputs, first_part.T, preferred_element_type=jnp.float32)).astype(jnp.bfloat16)
        group_part = jnp.dot(hidden, second_part, preferred_element_type=jnp.float32)
        return (running + group_part, None)
    projected, _ = lax.scan(one_group, jnp.zeros((NEWK, D), jnp.float32), (first_groups, second_groups))
    inverse_norm = lax.rsqrt(lax.optimization_barrier(jnp.sum(projected * projected, axis=1, keepdims=True)) + epsilon)
    return (projected * inverse_norm).astype(jnp.bfloat16)

def segment_logits(questions, segment):
    return inverse_temp * jnp.dot(questions, segment.T, preferred_element_type=jnp.float32)

def reference(key_inputs, head_in, head_out, queue_keys, slots, questions, positives):
    new_keys = encode_keys(key_inputs, head_in, head_out)
    queue_out = queue_keys.at[slots].set(new_keys)
    segments = queue_out.reshape(N_QUEUE, SEG_DEV, D)
    seg_starts = jnp.arange(N_QUEUE, dtype=jnp.int32) * SEG_DEV

    def statistics(carry, pair):
        row_top, row_total, pos_logit = carry
        segment, seg_start = pair
        logits = segment_logits(questions, segment)
        new_top = jnp.maximum(row_top, lax.optimization_barrier(jnp.max(logits, axis=1)))
        row_total = row_total * jnp.exp(row_top - new_top) + lax.optimization_barrier(jnp.sum(jnp.exp(logits - new_top[:, None]), axis=1))
        local_pos = positives - seg_start
        inside = (local_pos >= 0) & (local_pos < SEG_DEV)
        picked = jnp.take_along_axis(logits, jnp.clip(local_pos, 0, SEG_DEV - 1)[:, None], axis=1)[:, 0]
        pos_logit = pos_logit + jnp.where(inside, picked, jnp.zeros_like(picked))
        return ((new_top, row_total, pos_logit), None)
    start_carry = (jnp.full((QUES,), -jnp.inf, jnp.float32), jnp.zeros((QUES,), jnp.float32), jnp.zeros((QUES,), jnp.float32))
    (row_top, row_total, pos_logit), _ = lax.scan(statistics, start_carry, (segments, seg_starts))
    log_total = row_top + jnp.log(row_total)
    loss = jnp.mean(log_total - pos_logit)

    def gradients(running, pair):
        segment, seg_start = pair
        logits = segment_logits(questions, segment)
        weights = jnp.exp(logits - log_total[:, None]).astype(jnp.bfloat16)
        product = jnp.dot(weights, segment, preferred_element_type=jnp.float32)
        local_pos = positives - seg_start
        inside = (local_pos >= 0) & (local_pos < SEG_DEV)
        picked = segment[jnp.clip(local_pos, 0, SEG_DEV - 1)].astype(jnp.float32)
        term = inverse_temp * (product - jnp.where(inside[:, None], picked, jnp.zeros_like(picked)))
        return (running + term, None)
    question_grads, _ = lax.scan(gradients, jnp.zeros((QUES, D), jnp.float32), (segments, seg_starts))
    return (queue_out, loss, question_grads)
```

```python
import functools
import math

import jax
import jax.numpy as jnp
from jax import lax
from jax.experimental import pallas as pl
from jax.experimental.pallas import tpu as pltpu
from jax.sharding import PartitionSpec as P

inverse_temp = 20.0
epsilon = 1e-06
log2e = math.log2(math.e)
F32 = jnp.float32
BF16 = jnp.bfloat16
NEG = -1e30
CORES = 2
HALVES = 2


def nt_dot(a, b):
    return lax.dot_general(a, b, (((1,), (1,)), ((), ())), preferred_element_type=F32)


def dot(a, b):
    return jnp.dot(a, b, preferred_element_type=F32)


def iota(shape, axis):
    return lax.broadcasted_iota(jnp.int32, shape, axis)


def rcopy(src, dst, send, recv, device):
    return pltpu.make_async_remote_copy(
        src_ref=src,
        dst_ref=dst,
        send_sem=send,
        recv_sem=recv,
        device_id=device,
        device_id_type=pl.DeviceIdType.MESH,
    )


def peers(count, me, step):
    def one(d, carry):
        step(lax.rem(me + d, count))
        return carry

    lax.fori_loop(1, count, one, 0)


def row_to_col(row, eye):
    return jnp.sum(jnp.where(eye, row, 0.0), axis=1, keepdims=True)


def col_to_row(col, eye):
    return jnp.sum(jnp.where(eye, col, 0.0), axis=0, keepdims=True)


def kernel(
    nb, nq,
    x_hbm, win_hbm, wout_hbm, k_hbm, slots_hbm, q_hbm, pos_hbm,
    k_ref, loss_ref, grads_ref,
    slots_v, pos_v, x_v, win_v, wout_v, part_v, precv_v, q_v, nk_v, s_v, acc_v, pp_v,
    mx_v, slot_v, offrow_v, lp_v, sc_v, stats_v, psend_v, pairr_v, gsend_v, grecv_v, l1_v, l2_v,
    ld_sem, k_sem, w_send, w_recv, q_send, q_recv, qp_sem, p_send, p_recv, z_send, z_recv,
    st_send, st_recv, gp_sem, g_send, g_recv, l1_send, l1_recv, l2_send, l2_recv,
):
    z = lax.axis_index("batch")
    me = lax.axis_index("queue")
    chips = nq // CORES
    chip = me // CORES
    core = lax.rem(me, CORES)
    mate = (z, me + 1 - 2 * core)
    dim = x_v.shape[1]
    rows = x_v.shape[0]
    hid = win_hbm.shape[0]
    seg = k_ref.shape[0]
    nch, _, _, width = s_v.shape
    blocks = rows // nq
    sub = blocks // HALVES
    qrows = q_hbm.shape[0]
    half_q = chips * qrows
    ques = nq * qrows
    fresh = nb * blocks
    lanes = 128
    scale2 = inverse_temp * log2e

    def same_core(j):
        return (z, j * CORES + core)

    barrier = pltpu.get_barrier_semaphore()

    def greet(device):
        pl.semaphore_signal(barrier, inc=1, device_id=device, device_id_type=pl.DeviceIdType.MESH)

    peers(nq, me, lambda o: greet((z, o)))
    peers(nb, z, lambda o: greet((o, me)))

    my_in = win_v.at[pl.ds(pl.multiple_of(core * hid, hid), hid)]
    my_out = wout_v.at[pl.ds(pl.multiple_of(core * hid, hid), hid)]
    ld_slots = pltpu.make_async_copy(slots_hbm, slots_v, ld_sem.at[0])
    ld_pos = pltpu.make_async_copy(pos_hbm, pos_v, ld_sem.at[1])
    ld_x = pltpu.make_async_copy(x_hbm, x_v, ld_sem.at[2])
    ld_in = pltpu.make_async_copy(win_hbm, my_in, ld_sem.at[3])
    ld_out = pltpu.make_async_copy(wout_hbm, my_out, ld_sem.at[4])
    ld_q = pltpu.make_async_copy(q_hbm, q_v.at[core, chip], ld_sem.at[5])
    for load in (ld_slots, ld_pos, ld_x, ld_in, ld_out, ld_q):
        load.start()

    def ld_k(c):
        part = pl.ds(pl.multiple_of(c * width, width), width)
        return pltpu.make_async_copy(k_hbm.at[part], k_ref.at[part], k_sem.at[c])

    for c in range(nch):
        ld_k(c).start()

    ld_slots.wait()
    eye = iota((lanes, lanes), 0) == iota((lanes, lanes), 1)
    slot_shift = seg.bit_length() - 1
    block_shift = blocks.bit_length() - 1
    owner_all = lax.shift_right_logical(slots_v[...], slot_shift)
    local = jnp.where(owner_all == me, slots_v[...] - me * seg, 0)
    slot_rows = slots_v.shape[0]
    per_row = lanes // blocks
    spread = (
        lax.shift_right_logical(iota((fresh, slot_rows), 0), per_row.bit_length() - 1)
        == iota((fresh, slot_rows), 1)
    )
    spread = jnp.where(spread, 1.0, 0.0).astype(BF16)
    in_group = lax.shift_right_logical(iota((fresh, lanes), 1), block_shift) == (
        iota((fresh, lanes), 0) & (per_row - 1)
    )
    high = dot(spread, lax.shift_right_logical(local, 6).astype(F32).astype(BF16))
    low = dot(spread, (local & 63).astype(F32).astype(BF16))
    high = jnp.where(in_group, high, 0.0)
    low = jnp.where(in_group, low, 0.0)
    off_col = jnp.sum(high * 64.0 + low, axis=1, keepdims=True)
    ones = jnp.ones((8, lanes), BF16)
    offrow_v[...] = nt_dot(ones, high.astype(BF16)) * 64.0 + nt_dot(ones, low.astype(BF16))

    def mark(c, carry):
        ids = (iota((1, width), 1) + c * width).astype(F32)
        hit = jnp.sum(jnp.where(off_col == ids, 1.0, 0.0), axis=0, keepdims=True)
        slot_v[c] = jnp.where(hit > 0.5, -0.5, ids)
        return carry

    lax.fori_loop(0, nch, mark, 0)

    ld_pos.wait()
    pos_local = (pos_v[...] - me * seg).astype(F32)
    for a in range(ques // lanes):
        col = row_to_col(pos_local[a : a + 1, :], eye)
        for u in range(lanes // qrows):
            there = a * (lanes // qrows) + u
            lp_v[there % CORES, there // CORES] = jnp.broadcast_to(
                col[u * qrows : (u + 1) * qrows], (qrows, lanes)
            )

    z_rows = rows // lanes
    z_slots = slots_v[pl.ds(pl.multiple_of(z * z_rows, z_rows), z_rows), :]
    z_owner = lax.shift_right_logical(z_slots, slot_shift)

    def selection(h):
        i = iota((chips * sub, lanes), 0)
        sub_shift = sub.bit_length() - 1
        owner = lax.shift_right_logical(i, sub_shift) * CORES + core
        code = owner * blocks + (i & (sub - 1)) + h * sub
        pieces = []
        for r in range(z_rows):
            block = lax.shift_right_logical(iota((1, lanes), 1) + r * lanes, block_shift)
            pieces.append(
                jnp.where(code == z_owner[r : r + 1, :] * blocks + block, 1.0, 0.0).astype(BF16)
            )
        return jnp.concatenate(pieces, axis=1)

    ld_q.wait()
    pl.semaphore_wait(barrier, nq - 1 + nb - 1)

    w_copies = [
        rcopy(win_hbm, my_in, w_send.at[0], w_recv.at[0], mate),
        rcopy(wout_hbm, my_out, w_send.at[1], w_recv.at[1], mate),
    ]
    for copy in w_copies:
        copy.start()

    def q_copy(slot, target, index):
        return rcopy(
            q_hbm, q_v.at[core, slot], q_send.at[index], q_recv.at[slot], same_core(target)
        )

    peers(chips, chip, lambda j: q_copy(chip, j, j).start())

    ld_x.wait()
    ld_in.wait()
    ld_out.wait()

    def p_copy(h, slot, target, index):
        return rcopy(
            part_v.at[h, target],
            precv_v.at[h, slot],
            p_send.at[h, index],
            p_recv.at[h, slot],
            same_core(target),
        )

    for h in range(HALVES):
        chosen = dot(selection(h), x_v[...]).astype(BF16)
        if h == 0:
            for copy in w_copies:
                copy.wait_recv()
        hidden = jax.nn.gelu(nt_dot(chosen, win_v[...])).astype(BF16)
        part = dot(hidden, wout_v[...])
        part_v[h] = part.astype(BF16).reshape(chips, sub, dim)
        peers(chips, chip, lambda j: p_copy(h, chip, j, j).start())

    peers(chips, chip, lambda j: q_copy(j, j, j).wait_recv())
    qp_out = rcopy(q_v.at[core], q_v.at[core], qp_sem.at[0], qp_sem.at[1], mate)
    qp_in = rcopy(q_v.at[1 - core], q_v.at[1 - core], qp_sem.at[0], qp_sem.at[1], mate)
    qp_out.start()

    def old_logits(g, first):
        q = q_v[g].reshape(half_q, dim)
        lp = lp_v[g].reshape(half_q, lanes)[:, 0:1]
        pp_v[g] = jnp.zeros((half_q, dim), F32)
        mx_v[g] = jnp.full((half_q, lanes), NEG, F32)

        def one(c, carry):
            if first:
                ld_k(c).wait()
            keys = k_ref[pl.ds(pl.multiple_of(c * width, width), width), :]
            ids = slot_v[c]
            logit = jnp.where(ids >= 0.0, nt_dot(q, keys) * scale2, NEG)
            s_v[c, g] = logit
            top = logit[:, 0:lanes]
            for t in range(1, width // lanes):
                top = jnp.maximum(top, logit[:, t * lanes : (t + 1) * lanes])
            mx_v[g] = jnp.maximum(mx_v[g], top)
            pick = jnp.where(lp == ids, 1.0, 0.0).astype(BF16)
            pp_v[g] += dot(pick, keys)
            return carry

        lax.fori_loop(0, nch, one, 0)

    def z_copy(h, slot, target, index):
        return rcopy(
            nk_v.at[slot, h], nk_v.at[slot, h], z_send.at[h, index], z_recv.at[h, slot], (target, me)
        )

    def finish_keys(h):
        peers(chips, chip, lambda j: p_copy(h, j, j, j).wait_recv())

        def add(d, total):
            return total + precv_v[h, lax.rem(chip + d, chips)].astype(F32)

        total = lax.fori_loop(1, chips, add, part_v[h, chip].astype(F32))
        norm = lax.rsqrt(jnp.sum(total * total, axis=1, keepdims=True) + epsilon)
        nk_v[z, h] = (total * norm).astype(BF16)
        peers(nb, z, lambda o: z_copy(h, z, o, o).start())

    old_logits(core, True)
    finish_keys(0)
    qp_in.wait_recv()
    old_logits(1 - core, False)
    finish_keys(1)

    m_old = jnp.max(mx_v[...].reshape(ques, lanes), axis=1, keepdims=True)
    acc_v[...] = jnp.zeros(acc_v.shape, F32)
    mx_v[...] = jnp.zeros(mx_v.shape, F32)

    def old_product(c, carry):
        keys = k_ref[pl.ds(pl.multiple_of(c * width, width), width), :]
        weight = jnp.exp2(s_v[c].reshape(ques, width) - m_old)
        total = weight[:, 0:lanes]
        for t in range(1, width // lanes):
            total = total + weight[:, t * lanes : (t + 1) * lanes]
        mx_v[...] += total.reshape(mx_v.shape)
        acc_v[...] += dot(weight.astype(BF16), keys).reshape(acc_v.shape)
        return carry

    lax.fori_loop(0, nch, old_product, 0)
    l_old = jnp.sum(mx_v[...].reshape(ques, lanes), axis=1, keepdims=True)

    for h in range(HALVES):
        peers(nb, z, lambda o: z_copy(h, o, o, o).wait_recv())
    fresh_keys = nk_v[...].reshape(fresh, dim)
    q_all = q_v[...].reshape(ques, dim)
    new_logit = nt_dot(q_all, fresh_keys) * scale2
    m_all = jnp.maximum(m_old, jnp.max(new_logit, axis=1, keepdims=True))
    new_weight = jnp.exp2(new_logit - m_all)
    fade = jnp.exp2(m_old - m_all)
    l_all = l_old * fade + jnp.sum(new_weight, axis=1, keepdims=True)
    groups = ques // lanes
    for a in range(groups):
        stats_v[me, a : a + 1, :] = col_to_row(m_all[a * lanes : (a + 1) * lanes], eye)
        stats_v[me, groups + a : groups + a + 1, :] = col_to_row(
            l_all[a * lanes : (a + 1) * lanes], eye
        )

    def st_copy(slot, target, index):
        return rcopy(
            stats_v.at[slot], stats_v.at[slot], st_send.at[index], st_recv.at[slot], (z, target)
        )

    peers(nq, me, lambda o: st_copy(me, o, o).start())

    acc = acc_v[...].reshape(ques, dim) * fade + dot(new_weight.astype(BF16), fresh_keys)
    acc_v[...] = acc.reshape(acc_v.shape)
    lp_all = lp_v[...].reshape(ques, lanes)[:, 0:1]
    pick_new = jnp.where(lp_all == offrow_v[0:1, :], 1.0, 0.0).astype(BF16)
    pos_rows = pp_v[...].reshape(ques, dim) + dot(pick_new, fresh_keys)
    pp_v[...] = pos_rows.reshape(pp_v.shape)
    pos_sum = jnp.sum(jnp.sum(q_all.astype(F32) * pos_rows, axis=0, keepdims=True)) * scale2

    def update(c, carry):
        part = pl.ds(pl.multiple_of(c * width, width), width)
        ids = (iota((width, fresh), 0) + c * width).astype(F32)
        place = jnp.where(ids == offrow_v[0:1, :], 1.0, 0.0)
        hit = jnp.sum(place, axis=1, keepdims=True) > 0.5
        moved = dot(place.astype(BF16), fresh_keys)
        k_ref[part, :] = jnp.where(hit, moved, k_ref[part, :].astype(F32)).astype(BF16)
        return carry

    lax.fori_loop(0, nch // 2, update, 0)

    peers(nq, me, lambda o: st_copy(o, o, o).wait_recv())
    top = stats_v[0, 0:groups, :]
    for o in range(1, nq):
        top = jnp.maximum(top, stats_v[o, 0:groups, :])
    total = jnp.zeros_like(top)
    for o in range(nq):
        total = total + stats_v[o, groups : 2 * groups, :] * jnp.exp2(
            stats_v[o, 0:groups, :] - top
        )
    log_total = top + jnp.log(total) * log2e
    share = jnp.exp2(stats_v[me, 0:groups, :] - log_total) * inverse_temp
    for a in range(groups):
        col = row_to_col(share[a : a + 1, :], eye)
        first = a * lanes // half_q
        start = a * lanes - first * half_q
        sc_v[first, start : start + lanes, :] = jnp.broadcast_to(col, (lanes, lanes))
    own_loss = jnp.sum(log_total) * (1.0 / nq) - pos_sum
    l1_v[z] = jnp.broadcast_to(own_loss, (1, lanes))

    def l1_copy(slot, target, index):
        return rcopy(l1_v.at[slot], l1_v.at[slot], l1_send.at[index], l1_recv.at[slot], (target, me))

    def term(g):
        return acc_v[g] * sc_v[g][:, 0:1] - inverse_temp * pp_v[g]

    psend_v[...] = term(1 - core)
    pair = rcopy(psend_v, pairr_v, gp_sem.at[0], gp_sem.at[1], mate)
    pair.start()
    peers(nb, z, lambda o: l1_copy(z, o, o).start())
    acc_v[core] = term(core)
    pair.wait_recv()
    both = acc_v[core] + pairr_v[...]
    acc_v[core] = both
    gsend_v[...] = both.astype(BF16).reshape(gsend_v.shape)

    def g_copy(slot, target, index):
        return rcopy(
            gsend_v.at[target], grecv_v.at[slot], g_send.at[index], g_recv.at[slot],
            same_core(target),
        )

    peers(chips, chip, lambda j: g_copy(chip, j, j).start())

    peers(nb, z, lambda o: l1_copy(o, o, o).wait_recv())
    l2_v[me] = jnp.sum(l1_v[...], axis=0)

    def l2_copy(slot, target, index):
        return rcopy(l2_v.at[slot], l2_v.at[slot], l2_send.at[index], l2_recv.at[slot], (z, target))

    peers(nq, me, lambda o: l2_copy(me, o, o).start())

    lax.fori_loop(nch // 2, nch, update, 0)

    peers(chips, chip, lambda j: g_copy(j, j, j).wait_recv())

    def add_grads(d, total):
        return total + grecv_v[lax.rem(chip + d, chips)].astype(F32)

    own = acc_v[core, pl.ds(pl.multiple_of(chip * qrows, qrows), qrows), :]
    grads_ref[...] = lax.fori_loop(1, chips, add_grads, own)
    peers(nq, me, lambda o: l2_copy(o, o, o).wait_recv())
    loss_ref[...] = jnp.sum(l2_v[...], axis=0) * (1.0 / (log2e * ques * nb))

    for copy in w_copies:
        copy.wait_send()
    qp_out.wait_send()
    pair.wait_send()
    peers(chips, chip, lambda j: q_copy(chip, j, j).wait_send())
    for h in range(HALVES):
        peers(chips, chip, lambda j: p_copy(h, chip, j, j).wait_send())
        peers(nb, z, lambda o: z_copy(h, z, o, o).wait_send())
    peers(nq, me, lambda o: st_copy(me, o, o).wait_send())
    peers(chips, chip, lambda j: g_copy(chip, j, j).wait_send())
    peers(nb, z, lambda o: l1_copy(z, o, o).wait_send())
    peers(nq, me, lambda o: l2_copy(me, o, o).wait_send())


def body(key_inputs, head_in, head_out, queue_keys, slots, questions, positives):
    nb = lax.axis_size("batch")
    nq = lax.axis_size("queue")
    chips = nq // CORES
    rows, dim = key_inputs.shape
    hid = head_in.shape[0]
    seg = queue_keys.shape[0]
    qrows = questions.shape[0]
    half_q = chips * qrows
    ques = nq * qrows
    blocks = rows // nq
    sub = blocks // HALVES
    fresh = nb * blocks
    lanes = 128
    nch = 4
    width = seg // nch
    any_spec = pl.BlockSpec(memory_space=pl.ANY)
    vmem_spec = pl.BlockSpec(memory_space=pltpu.VMEM)
    dma = pltpu.SemaphoreType.DMA
    v = pltpu.VMEM
    queue_out, loss, grads = pl.pallas_call(
        functools.partial(kernel, nb, nq),
        out_shape=(
            jax.ShapeDtypeStruct((seg, dim), BF16),
            jax.ShapeDtypeStruct((1, lanes), F32),
            jax.ShapeDtypeStruct((qrows, dim), F32),
        ),
        in_specs=[any_spec] * 7,
        out_specs=(vmem_spec,) * 3,
        scratch_shapes=[
            v((nb * rows // lanes, lanes), jnp.int32),
            v((ques // lanes, lanes), jnp.int32),
            v((rows, dim), BF16),
            v((CORES * hid, dim), BF16),
            v((CORES * hid, dim), BF16),
            v((HALVES, chips, sub, dim), BF16),
            v((HALVES, chips, sub, dim), BF16),
            v((CORES, chips, qrows, dim), BF16),
            v((nb, HALVES, sub, dim), BF16),
            v((nch, CORES, half_q, width), F32),
            v((CORES, half_q, dim), F32),
            v((CORES, half_q, dim), F32),
            v((CORES, half_q, lanes), F32),
            v((nch, 1, width), F32),
            v((8, fresh), F32),
            v((CORES, chips, qrows, lanes), F32),
            v((CORES, half_q, lanes), F32),
            v((nq, 2 * ques // lanes, lanes), F32),
            v((half_q, dim), F32),
            v((half_q, dim), F32),
            v((chips, qrows, dim), BF16),
            v((chips, qrows, dim), BF16),
            v((nb, 1, lanes), F32),
            v((nq, 1, lanes), F32),
            dma((6,)),
            dma((nch,)),
            dma((2,)),
            dma((2,)),
            dma((chips,)),
            dma((chips,)),
            dma((2,)),
            dma((HALVES, chips)),
            dma((HALVES, chips)),
            dma((HALVES, nb)),
            dma((HALVES, nb)),
            dma((nq,)),
            dma((nq,)),
            dma((2,)),
            dma((chips,)),
            dma((chips,)),
            dma((nb,)),
            dma((nb,)),
            dma((nq,)),
            dma((nq,)),
        ],
        compiler_params=pltpu.CompilerParams(
            collective_id=0, has_side_effects=True, vmem_limit_bytes=58 * 1024 * 1024
        ),
        name="queue_step",
    )(
        key_inputs,
        head_in,
        head_out,
        queue_keys,
        slots.reshape(-1, lanes),
        questions,
        positives.reshape(-1, lanes),
    )
    return (queue_out, loss[0, 0], grads)


def solution(mesh):
    placed = (
        P("batch", None),
        P("queue", None),
        P("queue", None),
        P("queue", None),
        P(),
        P(("batch", "queue"), None),
        P("batch"),
    )
    return jax.shard_map(
        body,
        mesh=mesh,
        in_specs=placed,
        out_specs=(P("queue", None), P(), P(("batch", "queue"), None)),
        check_vma=False,
    )
```

```python
import functools
import math

import jax
import jax.numpy as jnp
from jax import lax
from jax.experimental import pallas as pl
from jax.experimental.pallas import tpu as pltpu
from jax.sharding import PartitionSpec as P

inverse_temp = 20.0
epsilon = 1e-06
log2e = math.log2(math.e)
F32 = jnp.float32
BF16 = jnp.bfloat16
NEG = -1e30
STEPS = 32700.0
TINY = 1e-30
CORES = 2
HALVES = 2


def nt_dot(a, b):
    return lax.dot_general(a, b, (((1,), (1,)), ((), ())), preferred_element_type=F32)


def dot(a, b):
    return jnp.dot(a, b, preferred_element_type=F32)


def iota(shape, axis):
    return lax.broadcasted_iota(jnp.int32, shape, axis)


def rcopy(src, dst, send, recv, device):
    return pltpu.make_async_remote_copy(
        src_ref=src,
        dst_ref=dst,
        send_sem=send,
        recv_sem=recv,
        device_id=device,
        device_id_type=pl.DeviceIdType.MESH,
    )


def peers(count, me, step):
    def one(d, carry):
        step(lax.rem(me + d, count))
        return carry

    lax.fori_loop(1, count, one, 0)


def row_to_col(row, eye):
    return jnp.sum(jnp.where(eye, row, 0.0), axis=1, keepdims=True)


def col_to_row(col, eye):
    return jnp.sum(jnp.where(eye, col, 0.0), axis=0, keepdims=True)


def kernel(
    nb, nq,
    x_hbm, win_hbm, wout_hbm, k_hbm, slots_hbm, q_hbm, pos_hbm,
    k_ref, loss_ref, grads_ref,
    slots_v, pos_v, x_v, win_v, wout_v, part_v, precv_v, q_v, nk_v, s_v, acc_v, pp_v,
    mx_v, slot_v, offrow_v, lp_v, sc_v, stats_v, psend_v, pairr_v, gsend_v, grecv_v, l1_v, l2_v, sel_v,
    ld_sem, k_sem, w_send, w_recv, q_send, q_recv, qp_sem, p_send, p_recv, z_send, z_recv,
    st_send, st_recv, gp_send, gp_recv, g_send, g_recv, l1_send, l1_recv, l2_send, l2_recv,
):
    z = lax.axis_index("batch")
    me = lax.axis_index("queue")
    chips = nq // CORES
    chip = me // CORES
    core = lax.rem(me, CORES)
    mate = (z, me + 1 - 2 * core)
    dim = x_v.shape[1]
    rows = x_v.shape[0]
    hid = win_hbm.shape[0]
    seg = k_ref.shape[0]
    nch, _, _, width = s_v.shape
    blocks = rows // nq
    sub = blocks // HALVES
    qrows = q_hbm.shape[0]
    half_q = chips * qrows
    ques = nq * qrows
    fresh = nb * blocks
    lanes = 128
    scale2 = inverse_temp * log2e

    def same_core(j):
        return (z, j * CORES + core)

    barrier = pltpu.get_barrier_semaphore()

    def greet(device):
        pl.semaphore_signal(barrier, inc=1, device_id=device, device_id_type=pl.DeviceIdType.MESH)

    peers(nq, me, lambda o: greet((z, o)))
    peers(nb, z, lambda o: greet((o, me)))

    my_in = win_v.at[pl.ds(pl.multiple_of(core * hid, hid), hid)]
    my_out = wout_v.at[pl.ds(pl.multiple_of(core * hid, hid), hid)]
    ld_slots = pltpu.make_async_copy(slots_hbm, slots_v, ld_sem.at[0])
    ld_pos = pltpu.make_async_copy(pos_hbm, pos_v, ld_sem.at[1])
    ld_x = pltpu.make_async_copy(x_hbm, x_v, ld_sem.at[2])
    ld_in = pltpu.make_async_copy(win_hbm, my_in, ld_sem.at[3])
    ld_out = pltpu.make_async_copy(wout_hbm, my_out, ld_sem.at[4])
    ld_q = pltpu.make_async_copy(q_hbm, q_v.at[core, chip], ld_sem.at[5])
    for load in (ld_slots, ld_pos, ld_x, ld_in, ld_out, ld_q):
        load.start()

    def ld_k(c):
        part = pl.ds(pl.multiple_of(c * width, width), width)
        return pltpu.make_async_copy(k_hbm.at[part], k_ref.at[part], k_sem.at[c])

    for c in range(nch):
        ld_k(c).start()

    ld_slots.wait()
    eye = iota((lanes, lanes), 0) == iota((lanes, lanes), 1)
    slot_shift = seg.bit_length() - 1
    block_shift = blocks.bit_length() - 1
    owner_all = lax.shift_right_logical(slots_v[...], slot_shift)
    local = jnp.where(owner_all == me, slots_v[...] - me * seg, 0)
    slot_rows = slots_v.shape[0]
    per_row = lanes // blocks
    spread = (
        lax.shift_right_logical(iota((fresh, slot_rows), 0), per_row.bit_length() - 1)
        == iota((fresh, slot_rows), 1)
    )
    spread = jnp.where(spread, 1.0, 0.0).astype(BF16)
    in_group = lax.shift_right_logical(iota((fresh, lanes), 1), block_shift) == (
        iota((fresh, lanes), 0) & (per_row - 1)
    )
    high = dot(spread, lax.shift_right_logical(local, 6).astype(F32).astype(BF16))
    low = dot(spread, (local & 63).astype(F32).astype(BF16))
    high = jnp.where(in_group, high, 0.0)
    low = jnp.where(in_group, low, 0.0)
    off_col = jnp.sum(high * 64.0 + low, axis=1, keepdims=True)
    ones = jnp.ones((8, lanes), BF16)
    offrow_v[...] = nt_dot(ones, high.astype(BF16)) * 64.0 + nt_dot(ones, low.astype(BF16))

    def mark(c, carry):
        ids = (iota((1, width), 1) + c * width).astype(F32)
        hit = jnp.sum(jnp.where(off_col == ids, 1.0, 0.0), axis=0, keepdims=True)
        slot_v[c] = jnp.where(hit > 0.5, -0.5, ids)
        return carry

    lax.fori_loop(0, nch, mark, 0)

    ld_pos.wait()
    pos_local = (pos_v[...] - me * seg).astype(F32)
    for a in range(ques // lanes):
        col = row_to_col(pos_local[a : a + 1, :], eye)
        for u in range(lanes // qrows):
            there = a * (lanes // qrows) + u
            lp_v[there % CORES, there // CORES] = jnp.broadcast_to(
                col[u * qrows : (u + 1) * qrows], (qrows, lanes)
            )

    z_rows = rows // lanes
    z_slots = slots_v[pl.ds(pl.multiple_of(z * z_rows, z_rows), z_rows), :]
    z_owner = lax.shift_right_logical(z_slots, slot_shift)

    def selection(h):
        i = iota((chips * sub, lanes), 0)
        sub_shift = sub.bit_length() - 1
        owner = lax.shift_right_logical(i, sub_shift) * CORES + core
        code = owner * blocks + (i & (sub - 1)) + h * sub
        pieces = []
        for r in range(z_rows):
            block = lax.shift_right_logical(iota((1, lanes), 1) + r * lanes, block_shift)
            pieces.append(
                jnp.where(code == z_owner[r : r + 1, :] * blocks + block, 1.0, 0.0).astype(BF16)
            )
        return jnp.concatenate(pieces, axis=1)

    ld_x.wait()
    for h in range(HALVES):
        sel_v[h] = dot(selection(h), x_v[...]).astype(BF16)
    chosen = sel_v[...].reshape(HALVES * chips * sub, dim)

    def head(index):
        units = pl.ds(pl.multiple_of(index * hid, hid), hid)
        hidden = jax.nn.gelu(nt_dot(chosen, win_v[units, :])).astype(BF16)
        return dot(hidden, wout_v[units, :])

    ld_in.wait()
    ld_out.wait()
    acc_v[...] = head(core).reshape(acc_v.shape)

    ld_q.wait()
    pl.semaphore_wait(barrier, nq - 1 + nb - 1)

    w_copies = [
        rcopy(win_hbm, my_in, w_send.at[0], w_recv.at[0], mate),
        rcopy(wout_hbm, my_out, w_send.at[1], w_recv.at[1], mate),
    ]
    for copy in w_copies:
        copy.start()

    def q_copy(slot, target, index):
        return rcopy(
            q_hbm, q_v.at[core, slot], q_send.at[index], q_recv.at[slot], same_core(target)
        )

    peers(chips, chip, lambda j: q_copy(chip, j, j).start())

    def p_copy(h, slot, target, index):
        return rcopy(
            part_v.at[h, target],
            precv_v.at[h, slot],
            p_send.at[h, index],
            p_recv.at[h, slot],
            same_core(target),
        )

    for copy in w_copies:
        copy.wait_recv()
    part = acc_v[...].reshape(HALVES * chips * sub, dim) + head(1 - core)
    most = jnp.maximum(jnp.max(jnp.abs(part), axis=1, keepdims=True), TINY)
    exponent = jnp.ceil(jnp.log(most) * log2e)
    coded = jnp.round(part * (jnp.exp2(-exponent) * STEPS)).astype(jnp.int32)
    part_v[:, :, :, 0:dim] = coded.astype(jnp.int16).reshape(HALVES, chips, sub, dim)
    tail = jnp.broadcast_to(exponent, (exponent.shape[0], lanes)).astype(jnp.int32)
    part_v[:, :, :, dim : dim + lanes] = tail.astype(jnp.int16).reshape(HALVES, chips, sub, lanes)
    for h in range(HALVES):
        peers(chips, chip, lambda j: p_copy(h, chip, j, j).start())

    lp_all = lp_v[...].reshape(ques, lanes)[:, 0:1]
    pp_v[...] = jnp.zeros(pp_v.shape, F32)

    def old_rows(c, carry):
        ld_k(c).wait()
        keys = k_ref[pl.ds(pl.multiple_of(c * width, width), width), :]
        pick = jnp.where(lp_all == slot_v[c], 1.0, 0.0).astype(BF16)
        pp_v[...] += dot(pick, keys).reshape(pp_v.shape)
        return carry

    lax.fori_loop(0, nch - 1, old_rows, 0)

    peers(chips, chip, lambda j: q_copy(j, j, j).wait_recv())
    qp_out = rcopy(q_v.at[core], q_v.at[core], qp_sem.at[0], qp_sem.at[1], mate)
    qp_in = rcopy(q_v.at[1 - core], q_v.at[1 - core], qp_sem.at[0], qp_sem.at[1], mate)
    qp_out.start()
    old_rows(nch - 1, 0)

    mx_v[...] = jnp.full(mx_v.shape, NEG, F32)

    def old_logits(g, start, stop):
        q = q_v[g].reshape(half_q, dim)

        def one(c, carry):
            keys = k_ref[pl.ds(pl.multiple_of(c * width, width), width), :]
            logit = jnp.where(slot_v[c] >= 0.0, nt_dot(q, keys) * scale2, NEG)
            s_v[c, g] = logit
            top = logit[:, 0:lanes]
            for t in range(1, width // lanes):
                top = jnp.maximum(top, logit[:, t * lanes : (t + 1) * lanes])
            mx_v[g] = jnp.maximum(mx_v[g], top)
            return carry

        lax.fori_loop(start, stop, one, 0)

    right = (lax.rem(z + 1, nb), me)
    left = (lax.rem(z + nb - 1, nb), me)
    reach = [(nb // 2, nb - 1 - nb // 2), (nb - 1 - nb // 2, nb // 2)]

    def z_copy(h, way, hop):
        away = (hop - 1) if way else (nb - hop + 1)
        slot = lax.rem(z + away, nb)
        there = nk_v.at[slot, h]
        return rcopy(
            there, there, z_send.at[h, way, hop - 1], z_recv.at[h, slot], left if way else right
        )

    def z_arrived(h, way, hop):
        slot = lax.rem(z + (hop if way else nb - hop), nb)
        there = nk_v.at[slot, h]
        rcopy(there, there, z_send.at[h, way, hop - 1], z_recv.at[h, slot], right).wait_recv()

    def z_step(h, hop):
        for way in range(2):
            if hop > 1 and hop - 1 <= reach[h][way]:
                z_arrived(h, way, hop - 1)
            if hop <= reach[h][way]:
                z_copy(h, way, hop).start()

    def finish_keys(h):
        peers(chips, chip, lambda j: p_copy(h, j, j, j).wait_recv())

        def decoded(ref, j):
            steps = ref[h, j, :, 0:dim].astype(jnp.int32).astype(F32)
            exponents = ref[h, j, :, dim : dim + lanes].astype(jnp.int32).astype(F32)
            return steps * (jnp.exp2(exponents[:, 0:1]) * (1.0 / STEPS))

        def add(d, total):
            return total + decoded(precv_v, lax.rem(chip + d, chips))

        total = lax.fori_loop(1, chips, add, decoded(part_v, chip))
        norm = lax.rsqrt(jnp.sum(total * total, axis=1, keepdims=True) + epsilon)
        nk_v[z, h] = (total * norm).astype(BF16)

    mid = nch // 2
    old_logits(core, 0, mid)
    finish_keys(0)
    z_step(0, 1)
    old_logits(core, mid, nch)
    z_step(0, 2)
    qp_in.wait_recv()
    old_logits(1 - core, 0, mid)
    finish_keys(1)
    z_step(1, 1)
    z_step(0, 3)
    old_logits(1 - core, mid, nch)
    z_step(1, 2)
    z_step(0, 4)

    m_old = jnp.max(mx_v[...].reshape(ques, lanes), axis=1, keepdims=True)
    acc_v[...] = jnp.zeros(acc_v.shape, F32)
    mx_v[...] = jnp.zeros(mx_v.shape, F32)

    def old_product(c, carry):
        keys = k_ref[pl.ds(pl.multiple_of(c * width, width), width), :]
        weight = jnp.exp2(s_v[c].reshape(ques, width) - m_old)
        total = weight[:, 0:lanes]
        for t in range(1, width // lanes):
            total = total + weight[:, t * lanes : (t + 1) * lanes]
        mx_v[...] += total.reshape(mx_v.shape)
        acc_v[...] += dot(weight.astype(BF16), keys).reshape(acc_v.shape)
        return carry

    old_product(0, 0)
    z_step(1, 3)
    z_step(0, 5)
    old_product(1, 0)
    z_step(1, 4)
    old_product(2, 0)
    z_step(1, 5)
    lax.fori_loop(3, nch, old_product, 0)
    l_old = jnp.sum(mx_v[...].reshape(ques, lanes), axis=1, keepdims=True)

    fresh_keys = nk_v[...].reshape(fresh, dim)
    q_all = q_v[...].reshape(ques, dim)
    new_logit = nt_dot(q_all, fresh_keys) * scale2
    m_all = jnp.maximum(m_old, jnp.max(new_logit, axis=1, keepdims=True))
    new_weight = jnp.exp2(new_logit - m_all)
    fade = jnp.exp2(m_old - m_all)
    l_all = l_old * fade + jnp.sum(new_weight, axis=1, keepdims=True)
    groups = ques // lanes
    for a in range(groups):
        stats_v[me, a : a + 1, :] = col_to_row(m_all[a * lanes : (a + 1) * lanes], eye)
        stats_v[me, groups + a : groups + a + 1, :] = col_to_row(
            l_all[a * lanes : (a + 1) * lanes], eye
        )

    def st_copy(slot, target, index):
        return rcopy(
            stats_v.at[slot], stats_v.at[slot], st_send.at[index], st_recv.at[slot], (z, target)
        )

    peers(nq, me, lambda o: st_copy(me, o, o).start())

    acc = acc_v[...].reshape(ques, dim) * fade + dot(new_weight.astype(BF16), fresh_keys)
    acc_v[...] = acc.reshape(acc_v.shape)
    pick_new = jnp.where(lp_all == offrow_v[0:1, :], 1.0, 0.0).astype(BF16)
    pos_rows = pp_v[...].reshape(ques, dim) + dot(pick_new, fresh_keys)
    pp_v[...] = pos_rows.reshape(pp_v.shape)
    pos_sum = jnp.sum(jnp.sum(q_all.astype(F32) * pos_rows, axis=0, keepdims=True)) * scale2

    def update(c, carry):
        part = pl.ds(pl.multiple_of(c * width, width), width)
        ids = (iota((width, fresh), 0) + c * width).astype(F32)
        place = jnp.where(ids == offrow_v[0:1, :], 1.0, 0.0)
        hit = jnp.sum(place, axis=1, keepdims=True) > 0.5
        moved = dot(place.astype(BF16), fresh_keys)
        k_ref[part, :] = jnp.where(hit, moved, k_ref[part, :].astype(F32)).astype(BF16)
        return carry

    lax.fori_loop(0, nch // 2, update, 0)

    peers(nq, me, lambda o: st_copy(o, o, o).wait_recv())
    top = stats_v[0, 0:groups, :]
    for o in range(1, nq):
        top = jnp.maximum(top, stats_v[o, 0:groups, :])
    total = jnp.zeros_like(top)
    for o in range(nq):
        total = total + stats_v[o, groups : 2 * groups, :] * jnp.exp2(
            stats_v[o, 0:groups, :] - top
        )
    log_total = top + jnp.log(total) * log2e
    share = jnp.exp2(stats_v[me, 0:groups, :] - log_total) * inverse_temp
    for a in range(groups):
        col = row_to_col(share[a : a + 1, :], eye)
        first = a * lanes // half_q
        start = a * lanes - first * half_q
        sc_v[first, start : start + lanes, :] = jnp.broadcast_to(col, (lanes, lanes))
    own_loss = jnp.sum(log_total) * (1.0 / nq) - pos_sum
    l1_v[z] = jnp.broadcast_to(own_loss, (1, lanes))

    def l1_copy(slot, target, index):
        return rcopy(l1_v.at[slot], l1_v.at[slot], l1_send.at[index], l1_recv.at[slot], (target, me))

    def term(g, d):
        part = pl.ds(pl.multiple_of(lax.rem(chip + d, chips) * qrows, qrows), qrows)
        return acc_v[g, part, :] * sc_v[g, part, 0:1] - inverse_temp * pp_v[g, part, :]

    def pair(half):
        part = pl.ds(half * (chips // 2), chips // 2)
        return rcopy(psend_v.at[part], pairr_v.at[part], gp_send.at[half], gp_recv.at[half], mate)

    def fill(d, carry):
        psend_v[d - 1] = term(1 - core, d)
        return carry

    for half in range(2):
        lax.fori_loop(half * (chips // 2) + 1, (half + 1) * (chips // 2) + 1, fill, 0)
        pair(half).start()
    peers(nb, z, lambda o: l1_copy(z, o, o).start())

    def g_copy(d, target, slot):
        return rcopy(
            gsend_v.at[d - 1], grecv_v.at[slot], g_send.at[d - 1], g_recv.at[slot],
            same_core(target),
        )

    def join(d, carry):
        gsend_v[d - 1] = (term(core, d) + pairr_v[d - 1]).astype(BF16)
        g_copy(d, lax.rem(chip + d, chips), chip).start()
        return carry

    pair(0).wait_recv()
    lax.fori_loop(1, chips // 2 + 1, join, 0)
    pair(1).wait_recv()
    lax.fori_loop(chips // 2 + 1, chips, join, 0)

    peers(nb, z, lambda o: l1_copy(o, o, o).wait_recv())
    l2_v[me] = jnp.sum(l1_v[...], axis=0)

    def l2_copy(slot, target, index):
        return rcopy(l2_v.at[slot], l2_v.at[slot], l2_send.at[index], l2_recv.at[slot], (z, target))

    peers(nq, me, lambda o: l2_copy(me, o, o).start())

    lax.fori_loop(nch // 2, nch, update, 0)

    peers(chips, chip, lambda j: g_copy(1, j, j).wait_recv())

    def add_grads(d, total):
        return total + grecv_v[lax.rem(chip + d, chips)].astype(F32)

    own = term(core, chips) + pairr_v[chips - 1]
    grads_ref[...] = lax.fori_loop(1, chips, add_grads, own)
    peers(nq, me, lambda o: l2_copy(o, o, o).wait_recv())
    loss_ref[...] = jnp.sum(l2_v[...], axis=0) * (1.0 / (log2e * ques * nb))

    for copy in w_copies:
        copy.wait_send()
    qp_out.wait_send()
    for half in range(2):
        pair(half).wait_send()
    peers(chips, chip, lambda j: q_copy(chip, j, j).wait_send())
    for h in range(HALVES):
        peers(chips, chip, lambda j: p_copy(h, chip, j, j).wait_send())
        for way in range(2):
            for hop in range(1, reach[h][way] + 1):
                z_copy(h, way, hop).wait_send()
    peers(nq, me, lambda o: st_copy(me, o, o).wait_send())

    def g_left(d, carry):
        g_copy(d, lax.rem(chip + d, chips), chip).wait_send()
        return carry

    lax.fori_loop(1, chips, g_left, 0)
    peers(nb, z, lambda o: l1_copy(z, o, o).wait_send())
    peers(nq, me, lambda o: l2_copy(me, o, o).wait_send())


def body(key_inputs, head_in, head_out, queue_keys, slots, questions, positives):
    nb = lax.axis_size("batch")
    nq = lax.axis_size("queue")
    chips = nq // CORES
    rows, dim = key_inputs.shape
    hid = head_in.shape[0]
    seg = queue_keys.shape[0]
    qrows = questions.shape[0]
    half_q = chips * qrows
    ques = nq * qrows
    blocks = rows // nq
    sub = blocks // HALVES
    fresh = nb * blocks
    lanes = 128
    nch = 4
    width = seg // nch
    any_spec = pl.BlockSpec(memory_space=pl.ANY)
    vmem_spec = pl.BlockSpec(memory_space=pltpu.VMEM)
    dma = pltpu.SemaphoreType.DMA
    v = pltpu.VMEM
    queue_out, loss, grads = pl.pallas_call(
        functools.partial(kernel, nb, nq),
        out_shape=(
            pltpu.VMEM((seg, dim), BF16),
            jax.ShapeDtypeStruct((1, lanes), F32),
            jax.ShapeDtypeStruct((qrows, dim), F32),
        ),
        in_specs=[any_spec] * 7,
        out_specs=(vmem_spec,) * 3,
        scratch_shapes=[
            v((nb * rows // lanes, lanes), jnp.int32),
            v((ques // lanes, lanes), jnp.int32),
            v((rows, dim), BF16),
            v((CORES * hid, dim), BF16),
            v((CORES * hid, dim), BF16),
            v((HALVES, chips, sub, dim + lanes), jnp.int16),
            v((HALVES, chips, sub, dim + lanes), jnp.int16),
            v((CORES, chips, qrows, dim), BF16),
            v((nb, HALVES, sub, dim), BF16),
            v((nch, CORES, half_q, width), F32),
            v((CORES, half_q, dim), F32),
            v((CORES, half_q, dim), F32),
            v((CORES, half_q, lanes), F32),
            v((nch, 1, width), F32),
            v((8, fresh), F32),
            v((CORES, chips, qrows, lanes), F32),
            v((CORES, half_q, lanes), F32),
            v((nq, 2 * ques // lanes, lanes), F32),
            v((chips, qrows, dim), F32),
            v((chips, qrows, dim), F32),
            v((chips, qrows, dim), BF16),
            v((chips, qrows, dim), BF16),
            v((nb, 1, lanes), F32),
            v((nq, 1, lanes), F32),
            v((HALVES, chips * sub, dim), BF16),
            dma((6,)),
            dma((nch,)),
            dma((2,)),
            dma((2,)),
            dma((chips,)),
            dma((chips,)),
            dma((2,)),
            dma((HALVES, chips)),
            dma((HALVES, chips)),
            dma((HALVES, 2, nb // 2)),
            dma((HALVES, nb)),
            dma((nq,)),
            dma((nq,)),
            dma((2,)),
            dma((2,)),
            dma((chips,)),
            dma((chips,)),
            dma((nb,)),
            dma((nb,)),
            dma((nq,)),
            dma((nq,)),
        ],
        compiler_params=pltpu.CompilerParams(
            collective_id=0, has_side_effects=True, vmem_limit_bytes=54 * 1024 * 1024
        ),
        name="queue_step",
    )(
        key_inputs,
        head_in,
        head_out,
        queue_keys,
        slots.reshape(-1, lanes),
        questions,
        positives.reshape(-1, lanes),
    )
    return (queue_out, loss[0, 0], grads)


def solution(mesh):
    placed = (
        P("batch", None),
        P("queue", None),
        P("queue", None),
        P("queue", None),
        P(),
        P(("batch", "queue"), None),
        P("batch"),
    )
    return jax.shard_map(
        body,
        mesh=mesh,
        in_specs=placed,
        out_specs=(P("queue", None), P(), P(("batch", "queue"), None)),
        check_vma=False,
    )
```

```python
import functools
import math

import jax
import jax.numpy as jnp
from jax import lax
from jax.experimental import pallas as pl
from jax.experimental.pallas import tpu as pltpu
from jax.sharding import PartitionSpec as P

inverse_temp = 20.0
epsilon = 1e-06
log2e = math.log2(math.e)
F32 = jnp.float32
BF16 = jnp.bfloat16
NEG = -1e30
STEPS = 32700.0
TINY = 1e-30
CORES = 2
HALVES = 2


def nt_dot(a, b):
    return lax.dot_general(a, b, (((1,), (1,)), ((), ())), preferred_element_type=F32)


def dot(a, b):
    return jnp.dot(a, b, preferred_element_type=F32)


def iota(shape, axis):
    return lax.broadcasted_iota(jnp.int32, shape, axis)


def rcopy(src, dst, send, recv, device):
    return pltpu.make_async_remote_copy(
        src_ref=src,
        dst_ref=dst,
        send_sem=send,
        recv_sem=recv,
        device_id=device,
        device_id_type=pl.DeviceIdType.MESH,
    )


def peers(count, me, step):
    def one(d, carry):
        step(lax.rem(me + d, count))
        return carry

    lax.fori_loop(1, count, one, 0)


def row_to_col(row, eye):
    return jnp.sum(jnp.where(eye, row, 0.0), axis=1, keepdims=True)


def col_to_row(col, eye):
    return jnp.sum(jnp.where(eye, col, 0.0), axis=0, keepdims=True)


def kernel(
    nb, nq,
    x_hbm, win_hbm, wout_hbm, k_hbm, slots_hbm, q_hbm, pos_hbm,
    k_ref, loss_ref, grads_ref,
    slots_v, pos_v, x_v, win_v, wout_v, part_v, precv_v, q_v, nk_v, s_v, acc_v, pp_v,
    mx_v, slot_v, offrow_v, lp_v, sc_v, stats_v, psend_v, pairr_v, gsend_v, grecv_v, l1_v, l2_v, sel_v, exp_v, hello_v,
    ld_sem, k_sem, w_send, w_recv, q_send, q_recv, qp_sem, p_send, p_recv, z_send, z_recv,
    st_send, st_recv, gp_send, gp_recv, g_send, g_recv, l1_send, l1_recv, l2_send, l2_recv,
    e_send, e_recv, hello_send, hello_recv,
):
    z = lax.axis_index("batch")
    me = lax.axis_index("queue")
    chips = nq // CORES
    chip = me // CORES
    core = lax.rem(me, CORES)
    mate = (z, me + 1 - 2 * core)
    dim = x_v.shape[1]
    rows = x_v.shape[0]
    hid = win_hbm.shape[0]
    seg = k_ref.shape[0]
    nch, _, _, width = s_v.shape
    blocks = rows // nq
    sub = blocks // HALVES
    qrows = q_hbm.shape[0]
    half_q = chips * qrows
    ques = nq * qrows
    fresh = nb * blocks
    lanes = 128
    scale2 = inverse_temp * log2e

    def same_core(j):
        return (z, j * CORES + core)

    barrier = pltpu.get_barrier_semaphore()

    def greet(device):
        pl.semaphore_signal(barrier, inc=1, device_id=device, device_id_type=pl.DeviceIdType.MESH)

    peers(nq, me, lambda o: greet((z, o)))
    peers(nb, z, lambda o: greet((o, me)))

    my_in = win_v.at[pl.ds(pl.multiple_of(core * hid, hid), hid)]
    my_out = wout_v.at[pl.ds(pl.multiple_of(core * hid, hid), hid)]
    ld_slots = pltpu.make_async_copy(slots_hbm, slots_v, ld_sem.at[0])
    ld_pos = pltpu.make_async_copy(pos_hbm, pos_v, ld_sem.at[1])
    ld_x = pltpu.make_async_copy(x_hbm, x_v, ld_sem.at[2])
    ld_in = pltpu.make_async_copy(win_hbm, my_in, ld_sem.at[3])
    ld_out = pltpu.make_async_copy(wout_hbm, my_out, ld_sem.at[4])
    ld_q = pltpu.make_async_copy(q_hbm, q_v.at[core, chip], ld_sem.at[5])
    for load in (ld_slots, ld_pos, ld_x, ld_in, ld_out, ld_q):
        load.start()

    def ld_k(c):
        part = pl.ds(pl.multiple_of(c * width, width), width)
        return pltpu.make_async_copy(k_hbm.at[part], k_ref.at[part], k_sem.at[c])

    for c in range(nch):
        ld_k(c).start()

    ld_slots.wait()
    eye = iota((lanes, lanes), 0) == iota((lanes, lanes), 1)
    slot_shift = seg.bit_length() - 1
    block_shift = blocks.bit_length() - 1
    owner_all = lax.shift_right_logical(slots_v[...], slot_shift)
    local = jnp.where(owner_all == me, slots_v[...] - me * seg, 0)
    slot_rows = slots_v.shape[0]
    per_row = lanes // blocks
    spread = (
        lax.shift_right_logical(iota((fresh, slot_rows), 0), per_row.bit_length() - 1)
        == iota((fresh, slot_rows), 1)
    )
    spread = jnp.where(spread, 1.0, 0.0).astype(BF16)
    in_group = lax.shift_right_logical(iota((fresh, lanes), 1), block_shift) == (
        iota((fresh, lanes), 0) & (per_row - 1)
    )
    high = dot(spread, lax.shift_right_logical(local, 6).astype(F32).astype(BF16))
    low = dot(spread, (local & 63).astype(F32).astype(BF16))
    high = jnp.where(in_group, high, 0.0)
    low = jnp.where(in_group, low, 0.0)
    off_col = jnp.sum(high * 64.0 + low, axis=1, keepdims=True)
    ones = jnp.ones((8, lanes), BF16)
    offrow_v[...] = nt_dot(ones, high.astype(BF16)) * 64.0 + nt_dot(ones, low.astype(BF16))

    def mark(c, carry):
        ids = (iota((1, width), 1) + c * width).astype(F32)
        hit = jnp.sum(jnp.where(off_col == ids, 1.0, 0.0), axis=0, keepdims=True)
        slot_v[c] = jnp.where(hit > 0.5, -0.5, ids)
        return carry

    lax.fori_loop(0, nch, mark, 0)

    ld_pos.wait()
    pos_local = (pos_v[...] - me * seg).astype(F32)
    for a in range(ques // lanes):
        col = row_to_col(pos_local[a : a + 1, :], eye)
        for u in range(lanes // qrows):
            there = a * (lanes // qrows) + u
            lp_v[there % CORES, there // CORES] = jnp.broadcast_to(
                col[u * qrows : (u + 1) * qrows], (qrows, lanes)
            )

    z_rows = rows // lanes
    z_slots = slots_v[pl.ds(pl.multiple_of(z * z_rows, z_rows), z_rows), :]
    z_owner = lax.shift_right_logical(z_slots, slot_shift)

    def selection(h):
        i = iota((chips * sub, lanes), 0)
        sub_shift = sub.bit_length() - 1
        owner = lax.shift_right_logical(i, sub_shift) * CORES + core
        code = owner * blocks + (i & (sub - 1)) + h * sub
        pieces = []
        for r in range(z_rows):
            block = lax.shift_right_logical(iota((1, lanes), 1) + r * lanes, block_shift)
            pieces.append(
                jnp.where(code == z_owner[r : r + 1, :] * blocks + block, 1.0, 0.0).astype(BF16)
            )
        return jnp.concatenate(pieces, axis=1)

    ld_x.wait()
    for h in range(HALVES):
        sel_v[h] = dot(selection(h), x_v[...]).astype(BF16)
    chosen = sel_v[...].reshape(HALVES * chips * sub, dim)

    def head(index):
        units = pl.ds(pl.multiple_of(index * hid, hid), hid)
        hidden = jax.nn.gelu(nt_dot(chosen, win_v[units, :])).astype(BF16)
        return dot(hidden, wout_v[units, :])

    ld_in.wait()
    ld_out.wait()
    acc_v[...] = head(core).reshape(acc_v.shape)

    ld_q.wait()
    pl.semaphore_wait(barrier, nq - 1 + nb - 1)

    w_copies = [
        rcopy(win_hbm, my_in, w_send.at[0], w_recv.at[0], mate),
        rcopy(wout_hbm, my_out, w_send.at[1], w_recv.at[1], mate),
    ]
    for copy in w_copies:
        copy.start()

    def hello(slot, target, index):
        return rcopy(
            hello_v.at[slot], hello_v.at[slot], hello_send.at[index], hello_recv.at[slot],
            (target, me),
        )

    def q_copy(slot, target, index):
        return rcopy(
            q_hbm, q_v.at[core, slot], q_send.at[index], q_recv.at[slot], same_core(target)
        )

    peers(chips, chip, lambda j: q_copy(chip, j, j).start())
    hello_v[z] = jnp.zeros((1, lanes), F32)
    peers(nb, z, lambda o: hello(z, o, o).start())

    def p_copy(h, slot, target, index):
        return rcopy(
            part_v.at[h, target],
            precv_v.at[h, slot],
            p_send.at[h, index],
            p_recv.at[h, slot],
            same_core(target),
        )

    for copy in w_copies:
        copy.wait_recv()
    part = acc_v[...].reshape(HALVES * chips * sub, dim) + head(1 - core)
    most = jnp.maximum(jnp.max(jnp.abs(part), axis=1, keepdims=True), TINY)
    exponent = jnp.ceil(jnp.log(most) * log2e)
    coded = jnp.round(part * (jnp.exp2(-exponent) * STEPS)).astype(jnp.int32)
    part_v[...] = coded.astype(jnp.int16).reshape(part_v.shape)
    for a in range(exp_v.shape[1]):
        exp_v[chip, a : a + 1, :] = col_to_row(exponent[a * lanes : (a + 1) * lanes], eye)

    def e_copy(slot, target, index):
        return rcopy(
            exp_v.at[slot], exp_v.at[slot], e_send.at[index], e_recv.at[slot], same_core(target)
        )

    peers(chips, chip, lambda j: e_copy(chip, j, j).start())
    for h in range(HALVES):
        peers(chips, chip, lambda j: p_copy(h, chip, j, j).start())

    lp_all = lp_v[...].reshape(ques, lanes)[:, 0:1]
    pp_v[...] = jnp.zeros(pp_v.shape, F32)

    def old_rows(c, carry):
        ld_k(c).wait()
        keys = k_ref[pl.ds(pl.multiple_of(c * width, width), width), :]
        pick = jnp.where(lp_all == slot_v[c], 1.0, 0.0).astype(BF16)
        pp_v[...] += dot(pick, keys).reshape(pp_v.shape)
        return carry

    lax.fori_loop(0, nch - 1, old_rows, 0)

    peers(chips, chip, lambda j: q_copy(j, j, j).wait_recv())
    qp_out = rcopy(q_v.at[core], q_v.at[core], qp_sem.at[0], qp_sem.at[1], mate)
    qp_in = rcopy(q_v.at[1 - core], q_v.at[1 - core], qp_sem.at[0], qp_sem.at[1], mate)
    qp_out.start()
    old_rows(nch - 1, 0)

    mx_v[...] = jnp.full(mx_v.shape, NEG, F32)

    def old_logits(g, start, stop):
        q = q_v[g].reshape(half_q, dim)

        def one(c, carry):
            keys = k_ref[pl.ds(pl.multiple_of(c * width, width), width), :]
            logit = jnp.where(slot_v[c] >= 0.0, nt_dot(q, keys) * scale2, NEG)
            s_v[c, g] = logit
            top = logit[:, 0:lanes]
            for t in range(1, width // lanes):
                top = jnp.maximum(top, logit[:, t * lanes : (t + 1) * lanes])
            mx_v[g] = jnp.maximum(mx_v[g], top)
            return carry

        lax.fori_loop(start, stop, one, 0)

    def z_copy(h, slot, target, index):
        there = nk_v.at[slot, h]
        return rcopy(there, there, z_send.at[h, index], z_recv.at[h, slot], (target, me))

    def finish_keys(h):
        if h == 0:
            peers(chips, chip, lambda j: e_copy(j, j, j).wait_recv())
        peers(chips, chip, lambda j: p_copy(h, j, j, j).wait_recv())

        place = h * chips * sub + chip * sub
        mine = iota((sub, lanes), 1) == iota((sub, lanes), 0) + lax.rem(place, lanes)

        def decoded(ref, j):
            row = exp_v[j, pl.ds(place // lanes, 1), :]
            factor = jnp.exp2(row_to_col(row, mine)) * (1.0 / STEPS)
            return ref[h, j].astype(jnp.int32).astype(F32) * factor

        def add(d, total):
            return total + decoded(precv_v, lax.rem(chip + d, chips))

        total = lax.fori_loop(1, chips, add, decoded(part_v, chip))
        norm = lax.rsqrt(jnp.sum(total * total, axis=1, keepdims=True) + epsilon)
        nk_v[z, h] = (total * norm).astype(BF16)
        peers(nb, z, lambda o: z_copy(h, z, o, o).start())

    old_logits(core, 0, nch)
    finish_keys(0)
    qp_in.wait_recv()
    old_logits(1 - core, 0, nch)

    m_old = jnp.max(mx_v[...].reshape(ques, lanes), axis=1, keepdims=True)
    acc_v[...] = jnp.zeros(acc_v.shape, F32)
    mx_v[...] = jnp.zeros(mx_v.shape, F32)

    def old_product(c, carry):
        keys = k_ref[pl.ds(pl.multiple_of(c * width, width), width), :]
        weight = jnp.exp2(s_v[c].reshape(ques, width) - m_old)
        total = weight[:, 0:lanes]
        for t in range(1, width // lanes):
            total = total + weight[:, t * lanes : (t + 1) * lanes]
        mx_v[...] += total.reshape(mx_v.shape)
        acc_v[...] += dot(weight.astype(BF16), keys).reshape(acc_v.shape)
        return carry

    mid = nch // 2
    lax.fori_loop(0, mid, old_product, 0)
    finish_keys(1)
    lax.fori_loop(mid, nch, old_product, 0)
    l_old = jnp.sum(mx_v[...].reshape(ques, lanes), axis=1, keepdims=True)

    for h in range(HALVES):
        peers(nb, z, lambda o: z_copy(h, o, o, o).wait_recv())
    fresh_keys = nk_v[...].reshape(fresh, dim)
    q_all = q_v[...].reshape(ques, dim)
    new_logit = nt_dot(q_all, fresh_keys) * scale2
    m_all = jnp.maximum(m_old, jnp.max(new_logit, axis=1, keepdims=True))
    new_weight = jnp.exp2(new_logit - m_all)
    fade = jnp.exp2(m_old - m_all)
    l_all = l_old * fade + jnp.sum(new_weight, axis=1, keepdims=True)
    groups = ques // lanes
    for a in range(groups):
        stats_v[me, a : a + 1, :] = col_to_row(m_all[a * lanes : (a + 1) * lanes], eye)
        stats_v[me, groups + a : groups + a + 1, :] = col_to_row(
            l_all[a * lanes : (a + 1) * lanes], eye
        )

    def st_copy(slot, target, index):
        return rcopy(
            stats_v.at[slot], stats_v.at[slot], st_send.at[index], st_recv.at[slot], (z, target)
        )

    peers(nq, me, lambda o: st_copy(me, o, o).start())

    acc = acc_v[...].reshape(ques, dim) * fade + dot(new_weight.astype(BF16), fresh_keys)
    acc_v[...] = acc.reshape(acc_v.shape)
    pick_new = jnp.where(lp_all == offrow_v[0:1, :], 1.0, 0.0).astype(BF16)
    pos_rows = pp_v[...].reshape(ques, dim) + dot(pick_new, fresh_keys)
    pp_v[...] = pos_rows.reshape(pp_v.shape)
    pos_sum = jnp.sum(jnp.sum(q_all.astype(F32) * pos_rows, axis=0, keepdims=True)) * scale2

    def update(c, carry):
        part = pl.ds(pl.multiple_of(c * width, width), width)
        ids = (iota((width, fresh), 0) + c * width).astype(F32)
        place = jnp.where(ids == offrow_v[0:1, :], 1.0, 0.0)
        hit = jnp.sum(place, axis=1, keepdims=True) > 0.5
        moved = dot(place.astype(BF16), fresh_keys)
        k_ref[part, :] = jnp.where(hit, moved, k_ref[part, :].astype(F32)).astype(BF16)
        return carry

    lax.fori_loop(0, nch // 2, update, 0)

    peers(nq, me, lambda o: st_copy(o, o, o).wait_recv())
    top = stats_v[0, 0:groups, :]
    for o in range(1, nq):
        top = jnp.maximum(top, stats_v[o, 0:groups, :])
    total = jnp.zeros_like(top)
    for o in range(nq):
        total = total + stats_v[o, groups : 2 * groups, :] * jnp.exp2(
            stats_v[o, 0:groups, :] - top
        )
    log_total = top + jnp.log(total) * log2e
    share = jnp.exp2(stats_v[me, 0:groups, :] - log_total) * inverse_temp
    for a in range(groups):
        col = row_to_col(share[a : a + 1, :], eye)
        first = a * lanes // half_q
        start = a * lanes - first * half_q
        sc_v[first, start : start + lanes, :] = jnp.broadcast_to(col, (lanes, lanes))
    own_loss = jnp.sum(log_total) * (1.0 / nq) - pos_sum
    l1_v[z] = jnp.broadcast_to(own_loss, (1, lanes))

    def l1_copy(slot, target, index):
        return rcopy(l1_v.at[slot], l1_v.at[slot], l1_send.at[index], l1_recv.at[slot], (target, me))

    def term(g, d):
        part = pl.ds(pl.multiple_of(lax.rem(chip + d, chips) * qrows, qrows), qrows)
        return acc_v[g, part, :] * sc_v[g, part, 0:1] - inverse_temp * pp_v[g, part, :]

    def pair(half):
        part = pl.ds(half * (chips // 2), chips // 2)
        return rcopy(psend_v.at[part], pairr_v.at[part], gp_send.at[half], gp_recv.at[half], mate)

    def fill(d, carry):
        psend_v[d - 1] = term(1 - core, d)
        return carry

    for half in range(2):
        first = half * (chips // 2) + 1
        lax.fori_loop(first, first + chips // 2, fill, 0, unroll=4)
        pair(half).start()
    peers(nb, z, lambda o: l1_copy(z, o, o).start())

    def g_copy(d, target, slot):
        return rcopy(
            gsend_v.at[d - 1], grecv_v.at[slot], g_send.at[d - 1], g_recv.at[slot],
            same_core(target),
        )

    def join(d, carry):
        gsend_v[d - 1] = (term(core, d) + pairr_v[d - 1]).astype(BF16)
        return carry

    def go(d, carry):
        g_copy(d, lax.rem(chip + d, chips), chip).start()
        return carry

    pair(0).wait_recv()
    lax.fori_loop(1, chips // 2 + 1, join, 0, unroll=4)
    lax.fori_loop(1, chips // 2 + 1, go, 0)
    pair(1).wait_recv()
    lax.fori_loop(chips // 2 + 1, chips + 1, join, 0, unroll=4)
    lax.fori_loop(chips // 2 + 1, chips, go, 0)

    peers(nb, z, lambda o: l1_copy(o, o, o).wait_recv())
    l2_v[me] = jnp.sum(l1_v[...], axis=0)

    def l2_copy(slot, target, index):
        return rcopy(l2_v.at[slot], l2_v.at[slot], l2_send.at[index], l2_recv.at[slot], (z, target))

    peers(nq, me, lambda o: l2_copy(me, o, o).start())

    lax.fori_loop(nch // 2, nch, update, 0)

    peers(chips, chip, lambda j: g_copy(1, j, j).wait_recv())

    def add_grads(d, total):
        return total + grecv_v[lax.rem(chip + d, chips)].astype(F32)

    own = term(core, chips) + pairr_v[chips - 1]
    grads_ref[...] = lax.fori_loop(1, chips, add_grads, own)
    peers(nq, me, lambda o: l2_copy(o, o, o).wait_recv())
    loss_ref[...] = jnp.sum(l2_v[...], axis=0) * (1.0 / (log2e * ques * nb))

    for copy in w_copies:
        copy.wait_send()
    qp_out.wait_send()
    for half in range(2):
        pair(half).wait_send()
    peers(chips, chip, lambda j: q_copy(chip, j, j).wait_send())
    peers(chips, chip, lambda j: e_copy(chip, j, j).wait_send())
    peers(nb, z, lambda o: hello(z, o, o).wait_send())
    peers(nb, z, lambda o: hello(o, o, o).wait_recv())
    for h in range(HALVES):
        peers(chips, chip, lambda j: p_copy(h, chip, j, j).wait_send())
        peers(nb, z, lambda o: z_copy(h, z, o, o).wait_send())
    peers(nq, me, lambda o: st_copy(me, o, o).wait_send())

    def g_left(d, carry):
        g_copy(d, lax.rem(chip + d, chips), chip).wait_send()
        return carry

    lax.fori_loop(1, chips, g_left, 0)
    peers(nb, z, lambda o: l1_copy(z, o, o).wait_send())
    peers(nq, me, lambda o: l2_copy(me, o, o).wait_send())


def body(key_inputs, head_in, head_out, queue_keys, slots, questions, positives):
    nb = lax.axis_size("batch")
    nq = lax.axis_size("queue")
    chips = nq // CORES
    rows, dim = key_inputs.shape
    hid = head_in.shape[0]
    seg = queue_keys.shape[0]
    qrows = questions.shape[0]
    half_q = chips * qrows
    ques = nq * qrows
    blocks = rows // nq
    sub = blocks // HALVES
    fresh = nb * blocks
    lanes = 128
    nch = 4
    width = seg // nch
    any_spec = pl.BlockSpec(memory_space=pl.ANY)
    vmem_spec = pl.BlockSpec(memory_space=pltpu.VMEM)
    dma = pltpu.SemaphoreType.DMA
    v = pltpu.VMEM
    queue_out, loss, grads = pl.pallas_call(
        functools.partial(kernel, nb, nq),
        out_shape=(
            pltpu.VMEM((seg, dim), BF16),
            jax.ShapeDtypeStruct((1, lanes), F32),
            jax.ShapeDtypeStruct((qrows, dim), F32),
        ),
        in_specs=[any_spec] * 7,
        out_specs=(vmem_spec,) * 3,
        scratch_shapes=[
            v((nb * rows // lanes, lanes), jnp.int32),
            v((ques // lanes, lanes), jnp.int32),
            v((rows, dim), BF16),
            v((CORES * hid, dim), BF16),
            v((CORES * hid, dim), BF16),
            v((HALVES, chips, sub, dim), jnp.int16),
            v((HALVES, chips, sub, dim), jnp.int16),
            v((CORES, chips, qrows, dim), BF16),
            v((nb, HALVES, sub, dim), BF16),
            v((nch, CORES, half_q, width), F32),
            v((CORES, half_q, dim), F32),
            v((CORES, half_q, dim), F32),
            v((CORES, half_q, lanes), F32),
            v((nch, 1, width), F32),
            v((8, fresh), F32),
            v((CORES, chips, qrows, lanes), F32),
            v((CORES, half_q, lanes), F32),
            v((nq, 2 * ques // lanes, lanes), F32),
            v((chips, qrows, dim), F32),
            v((chips, qrows, dim), F32),
            v((chips, qrows, dim), BF16),
            v((chips, qrows, dim), BF16),
            v((nb, 1, lanes), F32),
            v((nq, 1, lanes), F32),
            v((HALVES, chips * sub, dim), BF16),
            v((chips, HALVES * chips * sub // lanes, lanes), F32),
            v((nb, 1, lanes), F32),
            dma((6,)),
            dma((nch,)),
            dma((2,)),
            dma((2,)),
            dma((chips,)),
            dma((chips,)),
            dma((2,)),
            dma((HALVES, chips)),
            dma((HALVES, chips)),
            dma((HALVES, nb)),
            dma((HALVES, nb)),
            dma((nq,)),
            dma((nq,)),
            dma((2,)),
            dma((2,)),
            dma((chips,)),
            dma((chips,)),
            dma((nb,)),
            dma((nb,)),
            dma((nq,)),
            dma((nq,)),
            dma((chips,)),
            dma((chips,)),
            dma((nb,)),
            dma((nb,)),
        ],
        compiler_params=pltpu.CompilerParams(
            collective_id=0, has_side_effects=True, vmem_limit_bytes=54 * 1024 * 1024
        ),
        name="queue_step",
    )(
        key_inputs,
        head_in,
        head_out,
        queue_keys,
        slots.reshape(-1, lanes),
        questions,
        positives.reshape(-1, lanes),
    )
    return (queue_out, loss[0, 0], grads)


def solution(mesh):
    placed = (
        P("batch", None),
        P("queue", None),
        P("queue", None),
        P("queue", None),
        P(),
        P(("batch", "queue"), None),
        P("batch"),
    )
    return jax.shard_map(
        body,
        mesh=mesh,
        in_specs=placed,
        out_specs=(P("queue", None), P(), P(("batch", "queue"), None)),
        check_vma=False,
    )
```

```python
import functools
import math

import jax
import jax.numpy as jnp
from jax import lax
from jax.experimental import pallas as pl
from jax.experimental.pallas import tpu as pltpu
from jax.sharding import PartitionSpec as P

inverse_temp = 20.0
epsilon = 1e-06
log2e = math.log2(math.e)
F32 = jnp.float32
BF16 = jnp.bfloat16
NEG = -1e30
STEPS = 32700.0
TINY = 1e-30
CORES = 2
HALVES = 2


def nt_dot(a, b):
    return lax.dot_general(a, b, (((1,), (1,)), ((), ())), preferred_element_type=F32)


def dot(a, b):
    return jnp.dot(a, b, preferred_element_type=F32)


def iota(shape, axis):
    return lax.broadcasted_iota(jnp.int32, shape, axis)


def rcopy(src, dst, send, recv, device):
    return pltpu.make_async_remote_copy(
        src_ref=src,
        dst_ref=dst,
        send_sem=send,
        recv_sem=recv,
        device_id=device,
        device_id_type=pl.DeviceIdType.MESH,
    )


def peers(count, me, step):
    def one(d, carry):
        step(lax.rem(me + d, count))
        return carry

    lax.fori_loop(1, count, one, 0)


def row_to_col(row, eye):
    return jnp.sum(jnp.where(eye, row, 0.0), axis=1, keepdims=True)


def col_to_row(col, eye):
    return jnp.sum(jnp.where(eye, col, 0.0), axis=0, keepdims=True)


def kernel(
    nb, nq,
    x_hbm, win_hbm, wout_hbm, k_hbm, slots_hbm, q_hbm, pos_hbm,
    k_ref, loss_ref, grads_ref,
    slots_v, pos_v, x_v, win_v, wout_v, part_v, precv_v, q_v, nk_v, s_v, acc_v, pp_v,
    mx_v, slot_v, offrow_v, lp_v, sc_v, stats_v, psend_v, pairr_v, gsend_v, grecv_v, l1_v, l2_v, sel_v, exp_v, hello_v,
    ld_sem, k_sem, w_send, w_recv, q_send, q_recv, qp_sem, p_send, p_recv, z_send, z_recv,
    st_send, st_recv, gp_send, gp_recv, g_send, g_recv, l1_send, l1_recv, l2_send, l2_recv,
    e_send, e_recv, hello_send, hello_recv,
):
    z = lax.axis_index("batch")
    me = lax.axis_index("queue")
    chips = nq // CORES
    chip = me // CORES
    core = lax.rem(me, CORES)
    mate = (z, me + 1 - 2 * core)
    dim = x_v.shape[1]
    rows = x_v.shape[0]
    hid = win_hbm.shape[0]
    seg = k_ref.shape[0]
    nch, _, _, width = s_v.shape
    blocks = rows // nq
    sub = blocks // HALVES
    qrows = q_hbm.shape[0]
    half_q = chips * qrows
    ques = nq * qrows
    fresh = nb * blocks
    lanes = 128
    scale2 = inverse_temp * log2e

    def same_core(j):
        return (z, j * CORES + core)

    barrier = pltpu.get_barrier_semaphore()

    def greet(device):
        pl.semaphore_signal(barrier, inc=1, device_id=device, device_id_type=pl.DeviceIdType.MESH)

    peers(nq, me, lambda o: greet((z, o)))
    peers(nb, z, lambda o: greet((o, me)))

    my_in = win_v.at[pl.ds(pl.multiple_of(core * hid, hid), hid)]
    my_out = wout_v.at[pl.ds(pl.multiple_of(core * hid, hid), hid)]
    ld_slots = pltpu.make_async_copy(slots_hbm, slots_v, ld_sem.at[0])
    ld_pos = pltpu.make_async_copy(pos_hbm, pos_v, ld_sem.at[1])
    ld_x = pltpu.make_async_copy(x_hbm, x_v, ld_sem.at[2])
    ld_in = pltpu.make_async_copy(win_hbm, my_in, ld_sem.at[3])
    ld_out = pltpu.make_async_copy(wout_hbm, my_out, ld_sem.at[4])
    ld_q = pltpu.make_async_copy(q_hbm, q_v.at[core, chip], ld_sem.at[5])
    for load in (ld_slots, ld_pos, ld_x, ld_in, ld_out, ld_q):
        load.start()

    def ld_k(c):
        part = pl.ds(pl.multiple_of(c * width, width), width)
        return pltpu.make_async_copy(k_hbm.at[part], k_ref.at[part], k_sem.at[c])

    for c in range(nch):
        ld_k(c).start()

    ld_slots.wait()
    eye = iota((lanes, lanes), 0) == iota((lanes, lanes), 1)
    slot_shift = seg.bit_length() - 1
    block_shift = blocks.bit_length() - 1
    owner_all = lax.shift_right_logical(slots_v[...], slot_shift)
    local = jnp.where(owner_all == me, slots_v[...] - me * seg, 0)
    slot_rows = slots_v.shape[0]
    per_row = lanes // blocks
    spread = (
        lax.shift_right_logical(iota((fresh, slot_rows), 0), per_row.bit_length() - 1)
        == iota((fresh, slot_rows), 1)
    )
    spread = jnp.where(spread, 1.0, 0.0).astype(BF16)
    in_group = lax.shift_right_logical(iota((fresh, lanes), 1), block_shift) == (
        iota((fresh, lanes), 0) & (per_row - 1)
    )
    high = dot(spread, lax.shift_right_logical(local, 6).astype(F32).astype(BF16))
    low = dot(spread, (local & 63).astype(F32).astype(BF16))
    high = jnp.where(in_group, high, 0.0)
    low = jnp.where(in_group, low, 0.0)
    off_col = jnp.sum(high * 64.0 + low, axis=1, keepdims=True)
    ones = jnp.ones((8, lanes), BF16)
    offrow_v[...] = nt_dot(ones, high.astype(BF16)) * 64.0 + nt_dot(ones, low.astype(BF16))

    def mark(c, carry):
        ids = (iota((1, width), 1) + c * width).astype(F32)
        hit = jnp.sum(jnp.where(off_col == ids, 1.0, 0.0), axis=0, keepdims=True)
        slot_v[c] = jnp.where(hit > 0.5, -0.5, ids)
        return carry

    lax.fori_loop(0, nch, mark, 0)

    ld_pos.wait()
    pos_local = (pos_v[...] - me * seg).astype(F32)
    for a in range(ques // lanes):
        col = row_to_col(pos_local[a : a + 1, :], eye)
        for u in range(lanes // qrows):
            there = a * (lanes // qrows) + u
            lp_v[there % CORES, there // CORES] = jnp.broadcast_to(
                col[u * qrows : (u + 1) * qrows], (qrows, lanes)
            )

    z_rows = rows // lanes
    z_slots = slots_v[pl.ds(pl.multiple_of(z * z_rows, z_rows), z_rows), :]
    z_owner = lax.shift_right_logical(z_slots, slot_shift)

    def selection(h):
        i = iota((chips * sub, lanes), 0)
        sub_shift = sub.bit_length() - 1
        owner = lax.shift_right_logical(i, sub_shift) * CORES + core
        code = owner * blocks + (i & (sub - 1)) + h * sub
        pieces = []
        for r in range(z_rows):
            block = lax.shift_right_logical(iota((1, lanes), 1) + r * lanes, block_shift)
            pieces.append(
                jnp.where(code == z_owner[r : r + 1, :] * blocks + block, 1.0, 0.0).astype(BF16)
            )
        return jnp.concatenate(pieces, axis=1)

    ld_x.wait()
    for h in range(HALVES):
        sel_v[h] = dot(selection(h), x_v[...]).astype(BF16)
    chosen = sel_v[...].reshape(HALVES * chips * sub, dim)

    def head(index):
        units = pl.ds(pl.multiple_of(index * hid, hid), hid)
        hidden = jax.nn.gelu(nt_dot(chosen, win_v[units, :])).astype(BF16)
        return dot(hidden, wout_v[units, :])

    ld_in.wait()
    ld_out.wait()
    acc_v[...] = head(core).reshape(acc_v.shape)

    ld_q.wait()
    pl.semaphore_wait(barrier, nq - 1 + nb - 1)

    w_copies = [
        rcopy(win_hbm, my_in, w_send.at[0], w_recv.at[0], mate),
        rcopy(wout_hbm, my_out, w_send.at[1], w_recv.at[1], mate),
    ]
    for copy in w_copies:
        copy.start()

    def hello(slot, target, index):
        return rcopy(
            hello_v.at[slot], hello_v.at[slot], hello_send.at[index], hello_recv.at[slot],
            (target, me),
        )

    def q_copy(slot, target, index):
        return rcopy(
            q_hbm, q_v.at[core, slot], q_send.at[index], q_recv.at[slot], same_core(target)
        )

    peers(chips, chip, lambda j: q_copy(chip, j, j).start())
    hello_v[z] = jnp.zeros((1, lanes), F32)
    peers(nb, z, lambda o: hello(z, o, o).start())

    def p_copy(h, slot, target, index):
        return rcopy(
            part_v.at[h, target],
            precv_v.at[h, slot],
            p_send.at[h, index],
            p_recv.at[h, slot],
            same_core(target),
        )

    for copy in w_copies:
        copy.wait_recv()
    part = acc_v[...].reshape(HALVES * chips * sub, dim) + head(1 - core)
    most = jnp.maximum(jnp.max(jnp.abs(part), axis=1, keepdims=True), TINY)
    exponent = jnp.ceil(jnp.log(most) * log2e)
    coded = jnp.round(part * (jnp.exp2(-exponent) * STEPS)).astype(jnp.int32)
    part_v[...] = coded.astype(jnp.int16).reshape(part_v.shape)
    for a in range(exp_v.shape[1]):
        exp_v[chip, a : a + 1, :] = col_to_row(exponent[a * lanes : (a + 1) * lanes], eye)

    def e_copy(slot, target, index):
        return rcopy(
            exp_v.at[slot], exp_v.at[slot], e_send.at[index], e_recv.at[slot], same_core(target)
        )

    peers(chips, chip, lambda j: e_copy(chip, j, j).start())
    for h in range(HALVES):
        peers(chips, chip, lambda j: p_copy(h, chip, j, j).start())

    lp_all = lp_v[...].reshape(ques, lanes)[:, 0:1]
    pp_v[...] = jnp.zeros(pp_v.shape, F32)

    def old_rows(c, carry):
        ld_k(c).wait()
        keys = k_ref[pl.ds(pl.multiple_of(c * width, width), width), :]
        pick = jnp.where(lp_all == slot_v[c], 1.0, 0.0).astype(BF16)
        pp_v[...] += dot(pick, keys).reshape(pp_v.shape)
        return carry

    lax.fori_loop(0, nch - 1, old_rows, 0)

    peers(chips, chip, lambda j: q_copy(j, j, j).wait_recv())
    qp_out = rcopy(q_v.at[core], q_v.at[core], qp_sem.at[0], qp_sem.at[1], mate)
    qp_in = rcopy(q_v.at[1 - core], q_v.at[1 - core], qp_sem.at[0], qp_sem.at[1], mate)
    qp_out.start()
    old_rows(nch - 1, 0)

    mx_v[...] = jnp.full(mx_v.shape, NEG, F32)

    def old_logits(g, start, stop):
        q = q_v[g].reshape(half_q, dim)

        def one(c, carry):
            keys = k_ref[pl.ds(pl.multiple_of(c * width, width), width), :]
            logit = jnp.where(slot_v[c] >= 0.0, nt_dot(q, keys) * scale2, NEG)
            s_v[c, g] = logit
            top = logit[:, 0:lanes]
            for t in range(1, width // lanes):
                top = jnp.maximum(top, logit[:, t * lanes : (t + 1) * lanes])
            mx_v[g] = jnp.maximum(mx_v[g], top)
            return carry

        lax.fori_loop(start, stop, one, 0)

    def z_copy(h, slot, target, index):
        there = nk_v.at[slot, h]
        return rcopy(there, there, z_send.at[h, index], z_recv.at[h, slot], (target, me))

    def finish_keys(h):
        if h == 0:
            peers(chips, chip, lambda j: e_copy(j, j, j).wait_recv())
        peers(chips, chip, lambda j: p_copy(h, j, j, j).wait_recv())

        place = h * chips * sub + chip * sub
        mine = iota((sub, lanes), 1) == iota((sub, lanes), 0) + lax.rem(place, lanes)

        def decoded(ref, j):
            row = exp_v[j, pl.ds(place // lanes, 1), :]
            factor = jnp.exp2(row_to_col(row, mine)) * (1.0 / STEPS)
            return ref[h, j].astype(jnp.int32).astype(F32) * factor

        def add(d, total):
            return total + decoded(precv_v, lax.rem(chip + d, chips))

        total = lax.fori_loop(1, chips, add, decoded(part_v, chip))
        norm = lax.rsqrt(jnp.sum(total * total, axis=1, keepdims=True) + epsilon)
        nk_v[z, h] = (total * norm).astype(BF16)
        peers(nb, z, lambda o: z_copy(h, z, o, o).start())

    old_logits(core, 0, nch)
    finish_keys(0)
    qp_in.wait_recv()
    old_logits(1 - core, 0, nch)

    m_old = jnp.max(mx_v[...].reshape(ques, lanes), axis=1, keepdims=True)
    acc_v[...] = jnp.zeros(acc_v.shape, F32)
    mx_v[...] = jnp.zeros(mx_v.shape, F32)

    def old_product(c, carry):
        keys = k_ref[pl.ds(pl.multiple_of(c * width, width), width), :]
        weight = jnp.exp2(s_v[c].reshape(ques, width) - m_old)
        total = weight[:, 0:lanes]
        for t in range(1, width // lanes):
            total = total + weight[:, t * lanes : (t + 1) * lanes]
        mx_v[...] += total.reshape(mx_v.shape)
        acc_v[...] += dot(weight.astype(BF16), keys).reshape(acc_v.shape)
        return carry

    finish_keys(1)
    lax.fori_loop(0, nch, old_product, 0)
    l_old = jnp.sum(mx_v[...].reshape(ques, lanes), axis=1, keepdims=True)

    for h in range(HALVES):
        peers(nb, z, lambda o: z_copy(h, o, o, o).wait_recv())
    fresh_keys = nk_v[...].reshape(fresh, dim)
    q_all = q_v[...].reshape(ques, dim)
    new_logit = nt_dot(q_all, fresh_keys) * scale2
    m_all = jnp.maximum(m_old, jnp.max(new_logit, axis=1, keepdims=True))
    new_weight = jnp.exp2(new_logit - m_all)
    fade = jnp.exp2(m_old - m_all)
    l_all = l_old * fade + jnp.sum(new_weight, axis=1, keepdims=True)
    groups = ques // lanes
    for a in range(groups):
        stats_v[me, a : a + 1, :] = col_to_row(m_all[a * lanes : (a + 1) * lanes], eye)
        stats_v[me, groups + a : groups + a + 1, :] = col_to_row(
            l_all[a * lanes : (a + 1) * lanes], eye
        )

    def st_copy(slot, target, index):
        return rcopy(
            stats_v.at[slot], stats_v.at[slot], st_send.at[index], st_recv.at[slot], (z, target)
        )

    peers(nq, me, lambda o: st_copy(me, o, o).start())

    acc = acc_v[...].reshape(ques, dim) * fade + dot(new_weight.astype(BF16), fresh_keys)
    acc_v[...] = acc.reshape(acc_v.shape)
    pick_new = jnp.where(lp_all == offrow_v[0:1, :], 1.0, 0.0).astype(BF16)
    pos_rows = pp_v[...].reshape(ques, dim) + dot(pick_new, fresh_keys)
    pp_v[...] = pos_rows.reshape(pp_v.shape)
    pos_sum = jnp.sum(jnp.sum(q_all.astype(F32) * pos_rows, axis=0, keepdims=True)) * scale2

    def update(c, carry):
        part = pl.ds(pl.multiple_of(c * width, width), width)
        ids = (iota((width, fresh), 0) + c * width).astype(F32)
        place = jnp.where(ids == offrow_v[0:1, :], 1.0, 0.0)
        hit = jnp.sum(place, axis=1, keepdims=True) > 0.5
        moved = dot(place.astype(BF16), fresh_keys)
        k_ref[part, :] = jnp.where(hit, moved, k_ref[part, :].astype(F32)).astype(BF16)
        return carry

    lax.fori_loop(0, nch // 2, update, 0)

    peers(nq, me, lambda o: st_copy(o, o, o).wait_recv())
    top = stats_v[0, 0:groups, :]
    for o in range(1, nq):
        top = jnp.maximum(top, stats_v[o, 0:groups, :])
    total = jnp.zeros_like(top)
    for o in range(nq):
        total = total + stats_v[o, groups : 2 * groups, :] * jnp.exp2(
            stats_v[o, 0:groups, :] - top
        )
    log_total = top + jnp.log(total) * log2e
    share = jnp.exp2(stats_v[me, 0:groups, :] - log_total) * inverse_temp
    for a in range(groups):
        col = row_to_col(share[a : a + 1, :], eye)
        first = a * lanes // half_q
        start = a * lanes - first * half_q
        sc_v[first, start : start + lanes, :] = jnp.broadcast_to(col, (lanes, lanes))
    own_loss = jnp.sum(log_total) * (1.0 / nq) - pos_sum
    l1_v[z] = jnp.broadcast_to(own_loss, (1, lanes))

    def l1_copy(slot, target, index):
        return rcopy(l1_v.at[slot], l1_v.at[slot], l1_send.at[index], l1_recv.at[slot], (target, me))

    def term(g, d):
        part = pl.ds(pl.multiple_of(lax.rem(chip + d, chips) * qrows, qrows), qrows)
        return acc_v[g, part, :] * sc_v[g, part, 0:1] - inverse_temp * pp_v[g, part, :]

    def pair(half):
        part = pl.ds(half * (chips // 2), chips // 2)
        return rcopy(psend_v.at[part], pairr_v.at[part], gp_send.at[half], gp_recv.at[half], mate)

    def fill(d, carry):
        psend_v[d - 1] = term(1 - core, d)
        return carry

    for half in range(2):
        first = half * (chips // 2) + 1
        lax.fori_loop(first, first + chips // 2, fill, 0, unroll=4)
        pair(half).start()
    peers(nb, z, lambda o: l1_copy(z, o, o).start())

    def g_copy(d, target, slot):
        return rcopy(
            gsend_v.at[d - 1], grecv_v.at[slot], g_send.at[d - 1], g_recv.at[slot],
            same_core(target),
        )

    def join(d, carry):
        gsend_v[d - 1] = (term(core, d) + pairr_v[d - 1]).astype(BF16)
        return carry

    def go(d, carry):
        g_copy(d, lax.rem(chip + d, chips), chip).start()
        return carry

    pair(0).wait_recv()
    lax.fori_loop(1, chips // 2 + 1, join, 0, unroll=4)
    lax.fori_loop(1, chips // 2 + 1, go, 0)
    pair(1).wait_recv()
    lax.fori_loop(chips // 2 + 1, chips + 1, join, 0, unroll=4)
    lax.fori_loop(chips // 2 + 1, chips, go, 0)

    peers(nb, z, lambda o: l1_copy(o, o, o).wait_recv())
    l2_v[me] = jnp.sum(l1_v[...], axis=0)

    def l2_copy(slot, target, index):
        return rcopy(l2_v.at[slot], l2_v.at[slot], l2_send.at[index], l2_recv.at[slot], (z, target))

    peers(nq, me, lambda o: l2_copy(me, o, o).start())

    lax.fori_loop(nch // 2, nch, update, 0)

    peers(chips, chip, lambda j: g_copy(1, j, j).wait_recv())

    def add_grads(d, total):
        return total + grecv_v[lax.rem(chip + d, chips)].astype(F32)

    own = term(core, chips) + pairr_v[chips - 1]
    grads_ref[...] = lax.fori_loop(1, chips, add_grads, own)
    peers(nq, me, lambda o: l2_copy(o, o, o).wait_recv())
    loss_ref[...] = jnp.sum(l2_v[...], axis=0) * (1.0 / (log2e * ques * nb))

    for copy in w_copies:
        copy.wait_send()
    qp_out.wait_send()
    for half in range(2):
        pair(half).wait_send()
    peers(chips, chip, lambda j: q_copy(chip, j, j).wait_send())
    peers(chips, chip, lambda j: e_copy(chip, j, j).wait_send())
    peers(nb, z, lambda o: hello(z, o, o).wait_send())
    peers(nb, z, lambda o: hello(o, o, o).wait_recv())
    for h in range(HALVES):
        peers(chips, chip, lambda j: p_copy(h, chip, j, j).wait_send())
        peers(nb, z, lambda o: z_copy(h, z, o, o).wait_send())
    peers(nq, me, lambda o: st_copy(me, o, o).wait_send())

    def g_left(d, carry):
        g_copy(d, lax.rem(chip + d, chips), chip).wait_send()
        return carry

    lax.fori_loop(1, chips, g_left, 0)
    peers(nb, z, lambda o: l1_copy(z, o, o).wait_send())
    peers(nq, me, lambda o: l2_copy(me, o, o).wait_send())


def body(key_inputs, head_in, head_out, queue_keys, slots, questions, positives):
    nb = lax.axis_size("batch")
    nq = lax.axis_size("queue")
    chips = nq // CORES
    rows, dim = key_inputs.shape
    hid = head_in.shape[0]
    seg = queue_keys.shape[0]
    qrows = questions.shape[0]
    half_q = chips * qrows
    ques = nq * qrows
    blocks = rows // nq
    sub = blocks // HALVES
    fresh = nb * blocks
    lanes = 128
    nch = 4
    width = seg // nch
    any_spec = pl.BlockSpec(memory_space=pl.ANY)
    vmem_spec = pl.BlockSpec(memory_space=pltpu.VMEM)
    dma = pltpu.SemaphoreType.DMA
    v = pltpu.VMEM
    queue_out, loss, grads = pl.pallas_call(
        functools.partial(kernel, nb, nq),
        out_shape=(
            pltpu.VMEM((seg, dim), BF16),
            jax.ShapeDtypeStruct((1, lanes), F32),
            jax.ShapeDtypeStruct((qrows, dim), F32),
        ),
        in_specs=[any_spec] * 7,
        out_specs=(vmem_spec,) * 3,
        scratch_shapes=[
            v((nb * rows // lanes, lanes), jnp.int32),
            v((ques // lanes, lanes), jnp.int32),
            v((rows, dim), BF16),
            v((CORES * hid, dim), BF16),
            v((CORES * hid, dim), BF16),
            v((HALVES, chips, sub, dim), jnp.int16),
            v((HALVES, chips, sub, dim), jnp.int16),
            v((CORES, chips, qrows, dim), BF16),
            v((nb, HALVES, sub, dim), BF16),
            v((nch, CORES, half_q, width), F32),
            v((CORES, half_q, dim), F32),
            v((CORES, half_q, dim), F32),
            v((CORES, half_q, lanes), F32),
            v((nch, 1, width), F32),
            v((8, fresh), F32),
            v((CORES, chips, qrows, lanes), F32),
            v((CORES, half_q, lanes), F32),
            v((nq, 2 * ques // lanes, lanes), F32),
            v((chips, qrows, dim), F32),
            v((chips, qrows, dim), F32),
            v((chips, qrows, dim), BF16),
            v((chips, qrows, dim), BF16),
            v((nb, 1, lanes), F32),
            v((nq, 1, lanes), F32),
            v((HALVES, chips * sub, dim), BF16),
            v((chips, HALVES * chips * sub // lanes, lanes), F32),
            v((nb, 1, lanes), F32),
            dma((6,)),
            dma((nch,)),
            dma((2,)),
            dma((2,)),
            dma((chips,)),
            dma((chips,)),
            dma((2,)),
            dma((HALVES, chips)),
            dma((HALVES, chips)),
            dma((HALVES, nb)),
            dma((HALVES, nb)),
            dma((nq,)),
            dma((nq,)),
            dma((2,)),
            dma((2,)),
            dma((chips,)),
            dma((chips,)),
            dma((nb,)),
            dma((nb,)),
            dma((nq,)),
            dma((nq,)),
            dma((chips,)),
            dma((chips,)),
            dma((nb,)),
            dma((nb,)),
        ],
        compiler_params=pltpu.CompilerParams(
            collective_id=0, has_side_effects=True, vmem_limit_bytes=54 * 1024 * 1024
        ),
        name="queue_step",
    )(
        key_inputs,
        head_in,
        head_out,
        queue_keys,
        slots.reshape(-1, lanes),
        questions,
        positives.reshape(-1, lanes),
    )
    return (queue_out, loss[0, 0], grads)


def solution(mesh):
    placed = (
        P("batch", None),
        P("queue", None),
        P("queue", None),
        P("queue", None),
        P(),
        P(("batch", "queue"), None),
        P("batch"),
    )
    return jax.shard_map(
        body,
        mesh=mesh,
        in_specs=placed,
        out_specs=(P("queue", None), P(), P(("batch", "queue"), None)),
        check_vma=False,
    )
```
